128 devices in a mesh: row: 16 (over y_lo, x, core), col: 8 (over z, y_hi).
Axes of the slice: x: 4, y: 4 (y_hi: 2, y_lo: 2; y = y_hi * 2 + y_lo), z: 4, core: 2. Of those that a mesh axis runs over, the one named last changes fastest.
Arguments:
- series: bfloat16 [16384, 2048], P(('row', 'col')), may hold values from -6 to 6
- w_in: bfloat16 [2048, 1024], replicated, may hold values from -0.125 to 0.125
- w_out: bfloat16 [1024, 256], replicated, may hold values from -0.1875 to 0.1875
- factor_a: bfloat16 [16384, 32], P(('row', 'col')), may hold values from -3 to 3
- factor_b: bfloat16 [16384, 32], P(('row', 'col')), may hold values from -3 to 3
- mix_weight: float32 [8], replicated, may hold values from 0.2 to 2
- mix_var: float32 [8], replicated, may hold values from 0.0001 to 0.0006
- mix_mean: float32 [8, 256], replicated, may hold values from -0.0625 to 0.0625
Outputs:
- grad_embed: float32 [16384, 256], P(('row', 'col'))
- grad_in: float32 [2048, 1024], P('row', 'col')
- grad_out: float32 [1024, 256], P(('row', 'col'))
- grad_weight: float32 [8], replicated
- grad_var: float32 [8], replicated
- grad_mean: float32 [8, 256], replicated
The draws below stay inside these ranges and needn't reach their ends.
All inputs are finite; a program needn't handle non-finite values.
Results may differ from the reference program's by a relative error of at most 0.0067.
Values may be sent and summed in bfloat16 or wider, within the bound.
No kernel may reach another device: no remote copies, remote signals or barrier semaphores. Data moves between devices by JAX's collectives and lax.ppermute only.
A program may use at most 192 MiB of HBM per device.

```python
import math
import jax
import jax.numpy as jnp
from jax import lax

IN_DIM = 2048
HID = 1024
EMB = 256
COMP = 8
HALF_RANK = 32
ROWS_DEV = 128
TOKENS = 16384
N_COL = 8


def block_scale(key, dims, shards, least, largest):
    gain, own = 1.0, jax.random.fold_in(key, 6)
    for position, shards_of in shards:
        steps = jnp.exp(jax.random.uniform(jax.random.fold_in(own, position), (shards_of,), jnp.float32, least / len(shards), largest / len(shards)))
        gain = gain * jnp.repeat(steps, dims[position] // shards_of).reshape([-1 if axis == position else 1 for axis in range(len(dims))])
    return gain


def bell_draw(rng, shape, deviation, reach, pieces=(), held_as=jnp.bfloat16):
    entries = jax.random.normal(rng, shape, jnp.float32) * deviation
    if len(pieces) > 0:
        entries = block_scale(rng, shape, pieces, -0.22, 0.18) * entries
    return jnp.clip(entries, min=-reach, max=reach).astype(held_as)


def setup_inputs(seed: int = 0) -> dict:
    arg_keys = jax.random.split(jax.random.key(seed), 9)
    series = bell_draw(arg_keys[0], (TOKENS, IN_DIM), 1.0, 6.0, ((0, 128),))
    w_in = bell_draw(arg_keys[1], (IN_DIM, HID), IN_DIM ** -0.5, 0.125)
    w_out = bell_draw(arg_keys[2], (HID, EMB), HID ** -0.5, 0.1875)
    factor_a = bell_draw(arg_keys[3], (TOKENS, HALF_RANK), 0.2, 3.0, ((0, 128),))
    factor_b = bell_draw(arg_keys[4], (TOKENS, HALF_RANK), 0.2, 3.0, ((0, 128),))
    mix_weight = jnp.clip(jnp.exp(jax.random.uniform(arg_keys[5], (COMP,), jnp.float32, math.log(0.2), math.log(2.0))), 0.2, 2.0)
    mix_var = jnp.clip(jnp.exp(jax.random.uniform(arg_keys[6], (COMP,), jnp.float32, math.log(0.0001), math.log(0.0006))), 0.0001, 0.0006)
    mix_mean = bell_draw(arg_keys[7], (COMP, EMB), (40 * EMB) ** -0.5, 0.0625, (), jnp.float32)
    return dict(series=series, w_in=w_in, w_out=w_out, factor_a=factor_a, factor_b=factor_b, mix_weight=mix_weight, mix_var=mix_var, mix_mean=mix_mean)


two_pi = 2.0 * math.pi
two_pi_sq = 2.0 * math.pi * math.pi
highest = lax.Precision.HIGHEST


def tile_terms(row_e, row_f, col_e, col_f, row_cos, row_sin, col_cos, col_sin, mix_weight, mix_var):
    row_ef = row_e.astype(jnp.float32)
    col_ef = col_e.astype(jnp.float32)
    cross = lax.dot_general(row_e, col_e, (((1,), (1,)), ((), ())), preferred_element_type=jnp.float32)
    dist = jnp.sum(row_ef * row_ef, 1)[:, None] + jnp.sum(col_ef * col_ef, 1)[None, :] - 2.0 * cross
    outer = lax.dot_general(row_f, col_f, (((1,), (1,)), ((), ())), preferred_element_type=jnp.float32)
    coef = jnp.zeros_like(dist)
    spins = []
    weights = []
    varies = []
    for comp in range(mix_weight.shape[0]):
        rate = -two_pi_sq * mix_var[comp]
        damp = outer * jnp.exp(rate * dist)
        cosine = row_cos[comp][:, None] * col_cos[comp][None, :] + row_sin[comp][:, None] * col_sin[comp][None, :]
        even = damp * cosine
        coef = coef + (mix_weight[comp] * rate) * even
        weights.append(0.5 * jnp.sum(even))
        varies.append(0.5 * mix_weight[comp] * (-two_pi_sq) * jnp.sum(even * dist))
        with_cos = jnp.sum(damp * col_cos[comp][None, :], 1)
        with_sin = jnp.sum(damp * col_sin[comp][None, :], 1)
        spins.append(-two_pi * mix_weight[comp] * (row_sin[comp] * with_cos - row_cos[comp] * with_sin))
    rowsum = jnp.sum(coef, 1)
    pulled = jnp.dot(coef, col_ef, precision=highest)
    return rowsum, pulled, jnp.stack(spins, 0), jnp.stack(weights), jnp.stack(varies)


def reference(series, w_in, w_out, factor_a, factor_b, mix_weight, mix_var, mix_mean):
    pre = jnp.dot(series, w_in, preferred_element_type=jnp.float32)
    hidden = jax.nn.silu(pre).astype(jnp.bfloat16)
    emb = jnp.dot(hidden, w_out, preferred_element_type=jnp.float32).astype(jnp.bfloat16)
    emb_f = emb.astype(jnp.float32)
    left = jnp.concatenate([factor_a, factor_b], 1)
    right = jnp.concatenate([factor_b, factor_a], 1)
    phase = two_pi * lax.dot_general(mix_mean, emb_f, (((1,), (1,)), ((), ())), precision=highest)
    cosines = jnp.cos(phase)
    sines = jnp.sin(phase)
    block = ROWS_DEV * N_COL
    count = emb.shape[0] // block

    def one(start):
        row_e = lax.dynamic_slice_in_dim(emb, start, block, 0)
        row_f = lax.dynamic_slice_in_dim(left, start, block, 0)
        row_cos = lax.dynamic_slice_in_dim(cosines, start, block, 1)
        row_sin = lax.dynamic_slice_in_dim(sines, start, block, 1)
        rowsum, pulled, spin, weights, varies = tile_terms(row_e, row_f, emb, right, row_cos, row_sin, cosines, sines, mix_weight, mix_var)
        row_ef = row_e.astype(jnp.float32)
        grad = 2.0 * (rowsum[:, None] * row_ef - pulled) + lax.dot_general(spin, mix_mean, (((0,), (0,)), ((), ())), precision=highest)
        means = jnp.dot(spin, row_ef, precision=highest)
        return grad, means, weights, varies

    starts = jnp.arange(count, dtype=jnp.int32) * block
    grads, means, weights, varies = lax.map(one, starts)
    grad_embed = grads.reshape(emb.shape[0], emb.shape[1])
    grad_weight = jnp.sum(weights, 0)
    grad_var = jnp.sum(varies, 0)
    grad_mean = jnp.sum(means, 0)
    emb_cot = grad_embed.astype(jnp.bfloat16)
    back = lax.dot_general(emb_cot, w_out, (((1,), (1,)), ((), ())), preferred_element_type=jnp.float32)
    sigma = jax.nn.sigmoid(pre)
    d_hidden = (back * sigma * (1.0 + pre * (1.0 - sigma))).astype(jnp.bfloat16)
    grad_out = lax.dot_general(hidden, emb_cot, (((0,), (0,)), ((), ())), preferred_element_type=jnp.float32)
    grad_in = lax.dot_general(series, d_hidden, (((0,), (0,)), ((), ())), preferred_element_type=jnp.float32)
    return grad_embed, grad_in, grad_out, grad_weight, grad_var, grad_mean
```

```python
import functools
import math

import jax
import jax.numpy as jnp
import numpy as np
from jax import lax
from jax.experimental import pallas as pl
from jax.experimental.pallas import tpu as pltpu
from jax.sharding import PartitionSpec as P


f32, bf16 = jnp.float32, jnp.bfloat16
NT = (((1,), (1,)), ((), ()))
NN = (((1,), (0,)), ((), ()))


def mm(a, b, dims):
    return lax.dot_general(a, b, dims, preferred_element_type=f32)


def split(x, n):
    out = []
    for _ in range(n):
        h = lax.reduce_precision(x, 8, 7)
        out.append(h.astype(bf16))
        x = x - h
    return out


def rates(mix_var):
    return (-2 * math.pi**2 * math.log2(math.e)) * mix_var


HI = lax.Precision.HIGHEST
TN = (((0,), (0,)), ((), ()))


def sel_matrix():
    m = np.zeros((256, 128), np.float32)
    for q in range(8):
        for t, at in enumerate((64, 72, 88, 96)):
            m[16*(q//4) + 4*t + q%4, at+q] = 1
        m[32+q, 72+q] = 1; m[40+q, 80+q] = 1; m[48+q, 96+q] = 1; m[56+q, 104+q] = 1
    m[64:72, 112:115] = 1
    m[128+115:128+118, :] = 1
    return m


def prep2(emb, fa, fb, mw, mv, mmean):
    ef = emb.astype(f32)
    ang = 2*math.pi*lax.dot_general(ef, mmean, NT, precision=HI)
    c, s = jnp.cos(ang), jnp.sin(ang)
    n = jnp.sum(ef*ef, 1, keepdims=True)
    nh, nm, nl = split(n, 3)
    one = jnp.ones((emb.shape[0], 3), bf16)
    a = mw * (-2*math.pi**2) * mv
    ch, cl = split(c, 2); sh, sl = split(s, 2)
    ah, al = split(c*a, 2); bh, bl = split(s*a, 2)
    z = jnp.zeros((emb.shape[0], 10), bf16)
    colp = jnp.concatenate([emb*-2, fa, fb, ch, cl, ch, sh, sl, sh, nh, nm, nl, one, z], 1)
    rowp = jnp.concatenate([emb, fb, fa, ah, ah, al, bh, bh, bl, one, nh, nm, nl, z], 1)
    return rowp, colp


def tile_kernel(TS, CE2, TR, TC, final, n_prev, rate_ref, sel_ref, mean_ref, row_ref, col_ref, *refs):
    prev, outs = refs[:n_prev], refs[n_prev:]
    if final:
        grad_ref, means_ref, v_ref = outs[:3]
    else:
        pulled_ref, rsum_ref, cs_ref, v_ref = outs[:4]
    outs = outs[3 if final else 4:]
    (rowc_s, d0, d1, o0, o1, m0, m1, c0, c1, pulled_s, rsum_s, cs_s, cst_s, ni_s, nj_s) = outs
    HW = 128
    R, C = row_ref.shape[0], col_ref.shape[0]
    Q = rate_ref.shape[0]
    NC, NR = C // TC, R // TR
    N = NC * NR
    NS = TR // TS
    CW = min(TC, 256)
    lane = lax.broadcasted_iota(jnp.int32, (TS, 128), 1)

    def zero(*refs):
        for r in refs:
            r[...] = jnp.zeros_like(r)

    zero(d0, d1, o0, o1, m0, m1, c0, c1)
    if final:
        zero(means_ref)

    def load_sums(i):
        if prev:
            rows = pl.ds(pl.multiple_of(i * TR, TR), TR)
            pulled_s[...] = prev[0][rows, :]
            rsum_s[...] = prev[1][rows, :]
            cs_s[...] = prev[2][i]
        else:
            zero(pulled_s, rsum_s, cs_s)

    load_sums(0)
    if prev:
        v_ref[...] = prev[3][...]
    else:
        zero(v_ref)
    lr = lax.broadcasted_iota(jnp.int32, (TR, 128), 1)
    sub = lax.broadcasted_iota(jnp.int32, (16, TC), 0)

    def rowcol(t):
        t = jnp.clip(t, 0, N - 1)
        i, j = lax.div(t, NC), lax.rem(t, NC)
        return pl.multiple_of(i * TR, TR), pl.multiple_of(j * TC, TC)

    def products(t, d_s, o_s):
        r0, q0 = rowcol(t)
        cols = pl.ds(q0, TC)
        rows = pl.ds(r0, TR)

        def dist():
            norms = jnp.concatenate([ni_s[rows, :]] * (TC // 128), 1) + nj_s[0:1, cols]
            d_s[...] = norms + mm(row_ref[rows, :256], col_ref[cols, :256], NT)

        def outer():
            rtail = row_ref[rows, 256:384]
            keep = jnp.where((lr < 64) & (t < N), rtail, jnp.zeros_like(rtail))
            o_s[...] = mm(keep, col_ref[cols, 256:384], NT)

        return [dist, outer]

    def sums(t, damp_s, c_s):
        _, q0 = rowcol(t)
        cols = pl.ds(q0, TC)
        acc = [None, None]

        def waves(q):
            r = mm(cst_s[q, :, cols], damp_s[q], NT)
            h = q // 4
            acc[h] = r if acc[h] is None else acc[h] + r
            if q % 4 == 3:
                cs_s[16*h:16*h+16] += acc[h]

        def pull(h):
            M = TR
            rows = slice(h * M, (h + 1) * M)
            emb = col_ref[cols, :256]
            c = c_s[rows, :]
            chi = c.astype(bf16)
            pu = mm(chi, emb, NN)
            if CE2:
                pu = pu + mm((c - chi.astype(f32)).astype(bf16), emb, NN)
            pulled_s[rows, :] += pu
            rs = c[:, :128]
            for k in range(1, TC // 128):
                rs = rs + c[:, k*128:(k+1)*128]
            rsum_s[rows, :] += rs

        return [functools.partial(waves, q) for q in range(Q)], [functools.partial(pull, h) for h in range(1)]

    def stage(t, da, oa, ds, os, ms, cs, mc, cc_):
        first = products(t, da, oa)
        waves, pulls = sums(t - 2, mc, cc_)
        r0, q0 = rowcol(t - 1)
        for s in range(NS):
            rs = slice(s * TS, (s + 1) * TS)
            lhs = rowc_s[pl.ds(pl.multiple_of((r0 + s * TS) * Q, TS * Q), Q*TS), :]
            for cc in range(TC // CW):
                cos = mm(lhs, col_ref[pl.ds(q0 + cc*CW, CW), 256:384], NT)
                for hh in range(CW // HW):
                    sl = slice(hh*HW, (hh+1)*HW)
                    hcols = slice(cc*CW + hh*HW, cc*CW + (hh+1)*HW)
                    d = ds[rs, hcols]
                    o = os[rs, hcols]
                    c = None
                    for q in range(Q):
                        damp = o * jnp.exp2(d * rate_ref[q])
                        ms[q, rs, hcols] = damp.astype(bf16)
                        even = damp * cos[q*TS:(q+1)*TS, sl]
                        c = even if c is None else c + even
                        ed = even * d
                        x = ed[:, :128]
                        for k in range(1, HW // 128):
                            x = x + ed[:, k*128:(k+1)*128]
                        x = x.reshape(TS//8, 8, 128).sum(0)
                        v_ref[q] += x
                        v_ref[Q + q] += even.reshape(TS//8, 8, 128).sum(0)
                    cs[rs, hcols] = c
            for _ in range(-(-Q // NS)):
                if waves:
                    waves.pop(0)()
            if s % max(1, NS // 2) == 0 and first:
                first.pop(0)()
            if (s % max(1, NS // 2) == 1 or NS == 2) and pulls:
                pulls.pop(0)()
        for f in first + waves + pulls:
            f()

    def end_rows(t):
        @pl.when((t >= 0) & (lax.rem(t, NC) == NC - 1))
        def _():
            r0, _ = rowcol(t)
            rows = pl.ds(r0, TR)
            if final:
                ef = row_ref[rows, :256].astype(f32)
                cs = cs_s[...]
                wc = jnp.concatenate([cs[0:4] + cs[4:8], cs[16:20] + cs[20:24]], 0)
                ws = jnp.concatenate([cs[8:12] + cs[12:16], cs[24:28] + cs[28:32]], 0)
                rt = mm(sel_ref[32:64], row_ref[rows, 256:384], NT)
                ac = rt[0:8] + rt[8:16]
                as_ = rt[16:24] + rt[24:32]
                spin = as_ * wc - ac * ws
                rowsum = jnp.sum(rsum_s[...], 1, keepdims=True)
                back = lax.dot_general(spin, mean_ref[...], TN, precision=HI, preferred_element_type=f32)
                grad_ref[rows, :] = (2.0 * rowsum * ef + pulled_s[...] + back).astype(grad_ref.dtype)
                means_ref[...] += lax.dot_general(spin, ef, NN, precision=HI, preferred_element_type=f32)
            else:
                pulled_ref[rows, :] = pulled_s[...]
                rsum_ref[rows, :] = rsum_s[...]
                cs_ref[lax.div(t, NC)] = cs_s[...]
            load_sums(jnp.minimum(lax.div(t, NC) + 1, NR - 1))

    for s in range(R // TS):
        x = row_ref[s*TS:(s+1)*TS, 256:384]
        for q in range(Q):
            keep = (lane >= 64) & (lane < 112) & (lane % 8 == q)
            rowc_s[(s*Q+q)*TS:(s*Q+q+1)*TS, :] = jnp.where(keep, x, jnp.zeros_like(x))
    for k in range(C // TC):
        cst = mm(sel_ref[:32], col_ref[k*TC:(k+1)*TC, 256:384], NT)
        for q in range(Q):
            keep = cst[16*(q//4):16*(q//4)+16]
            cst_s[q, :, k*TC:(k+1)*TC] = jnp.where(sub % 4 == q % 4, keep, 0.0).astype(bf16)
        nj_s[:, k*TC:(k+1)*TC] = mm(sel_ref[64:72], col_ref[k*TC:(k+1)*TC, 256:384], NT)
    for k in range(R // TR):
        ni_s[k*TR:(k+1)*TR, :] = mm(row_ref[k*TR:(k+1)*TR, 256:384], sel_ref[128:256], NN)

    def pair(h, _):
        t = 2 * h
        stage(t, d0, o0, d1, o1, m1, c1, m0, c0)
        stage(t + 1, d1, o1, d0, o0, m0, c0, m1, c1)
        end_rows(t - 1)
        return 0

    lax.fori_loop(0, (N + 2) // 2, pair, 0)


def tile(rate, mean_s, rowp, colp, prev=(), final=True, TR=256, TC=256, TS=64, CE2=False):
    R, C, Q = rowp.shape[0], colp.shape[0], rate.shape[0]
    assert (R // TR) * (C // TC) % 2 == 0
    vm = pl.BlockSpec(memory_space=pltpu.VMEM)
    sc = lambda *s: pltpu.VMEM(s, f32)
    shape = lambda *dims: jax.ShapeDtypeStruct(dims, f32)
    if final:
        shapes = [shape(R, 256), shape(8, 256), shape(2 * Q, 8, 128)]
    else:
        shapes = [shape(R, 256), shape(R, 128), shape(R // TR, 32, TR), shape(2 * Q, 8, 128)]
    return pl.pallas_call(
        functools.partial(tile_kernel, TS, CE2, TR, TC, final, len(prev)),
        in_specs=[pl.BlockSpec(memory_space=pltpu.SMEM), vm, vm, vm, vm] + [vm] * len(prev),
        out_specs=[vm] * len(shapes),
        out_shape=shapes,
        scratch_shapes=[pltpu.VMEM((R*Q, 128), bf16), sc(TR, TC), sc(TR, TC), sc(TR, TC), sc(TR, TC),
                        pltpu.VMEM((Q, TR, TC), bf16), pltpu.VMEM((Q, TR, TC), bf16), sc(TR, TC), sc(TR, TC),
                        sc(TR, 256), sc(TR, 128), sc(32, TR), pltpu.VMEM((Q, 16, C), bf16), sc(R, 128), sc(8, C)],
        cost_estimate=pl.CostEstimate(flops=20 * R * C * 256, bytes_accessed=4 * 10**6, transcendentals=R * C * Q),
        compiler_params=pltpu.CompilerParams(vmem_limit_bytes=20 << 20),
        name="tile",
    )(rate, jnp.asarray(sel_matrix(), bf16), mean_s, rowp, colp, *prev)


def pre_kernel(w_ref, wh_ref, *refs):
    pieces, (slope_ref, hid_ref) = refs[:-2], refs[-2:]
    for p in range(0, len(pieces), 2):
        two = jnp.concatenate([pieces[p][...], pieces[p+1][...]], 0)
        n = two.shape[0]
        cols = slice(p * n // 2, (p + 2) * n // 2)
        pre = mm(two, w_ref[...], NN)
        sig = jax.nn.sigmoid(pre)
        slope_ref[:, cols] = (sig * (1.0 + pre * (1.0 - sig))).T
        pre = mm(two, wh_ref[...], NN)
        hid_ref[:, cols] = (pre * jax.nn.sigmoid(pre)).T.astype(bf16)


def late_pre(w_own, w_pick, pieces):
    vm = pl.BlockSpec(memory_space=pltpu.VMEM)
    tok = sum(p.shape[0] for p in pieces)
    return pl.pallas_call(
        pre_kernel,
        in_specs=[vm] * (2 + len(pieces)),
        out_specs=[vm, vm],
        out_shape=[jax.ShapeDtypeStruct((w_own.shape[1], tok), f32), jax.ShapeDtypeStruct((w_pick.shape[1], tok), bf16)],
        cost_estimate=pl.CostEstimate(flops=4 * 10**9, bytes_accessed=6 * 10**6, transcendentals=400000),
        compiler_params=pltpu.CompilerParams(vmem_limit_bytes=20 << 20),
        name="pre",
    )(w_own, w_pick, *pieces)


def pair_split(x):
    h = x.astype(bf16)
    return h, (x - h.astype(f32)).astype(bf16)


def part_kernel(own, n, at_ref, slope_ref, hid_ref, w_ref, *refs):
    cots, pieces, (out_ref,) = refs[:n], refs[n:2*n], refs[2*n:]
    core, x, y, z = at_ref[0], at_ref[1], at_ref[2], at_ref[3]
    wide = slope_ref.shape[0]
    cot = jnp.concatenate([c[:own, :] for c in cots], 0)
    small = cots[0][own:own+16, :].astype(f32) + cots[0][own+16:own+32, :].astype(f32)
    for c in cots[1:]:
        small = small + (c[own:own+16, :].astype(f32) + c[own+16:own+32, :].astype(f32))
    hi, lo = pair_split(small)
    for k, part in enumerate((hi, lo)):
        for dest in range(4):
            out_ref[dest, 576+32*k:592+32*k, :] = part[:, :128]
            out_ref[dest, 592+32*k:608+32*k, :] = part[:, 128:]
    back = mm(w_ref[pl.ds(pl.multiple_of(z * wide, wide), wide), :], cot, NT)
    d = (back * slope_ref[...]).astype(bf16)
    grad_out = mm(hid_ref[...], cot, NN)
    for m in range(8):
        feats = pl.ds(pl.multiple_of((2 * m + core) * 128, 128), 128)
        g = mm(d, jnp.concatenate([p[:, feats] for p in pieces], 0), NN)
        sx = lax.rem(m % 4 - x + 4, 4)
        for h in range(2):
            sy = lax.rem(2 * h + m // 4 - y + 4, 4)
            base = pl.multiple_of(sy * 144, 16)
            out_ref[sx, pl.ds(base, 128), :] = g[h*128:(h+1)*128].astype(bf16)
            o = grad_out[16*m+8*h:16*m+8*h+8]
            out_ref[sx, pl.ds(base + 128, 16), :] = jnp.concatenate([o[:, :128], o[:, 128:]], 0).astype(bf16)


def late_part(at, slope, hid_out, w_out, cots, pieces):
    vm = pl.BlockSpec(memory_space=pltpu.VMEM)
    n = len(pieces)
    return pl.pallas_call(
        functools.partial(part_kernel, pieces[0].shape[0], n),
        in_specs=[pl.BlockSpec(memory_space=pltpu.SMEM)] + [vm] * (3 + 2 * n),
        out_specs=vm,
        out_shape=jax.ShapeDtypeStruct((4, 640, 128), bf16),
        cost_estimate=pl.CostEstimate(flops=2 * 10**9, bytes_accessed=6 * 10**6, transcendentals=0),
        compiler_params=pltpu.CompilerParams(vmem_limit_bytes=20 << 20),
        name="part",
    )(at, slope, hid_out, w_out, *cots, *pieces)


def add_kernel(first_ref, *refs):
    got, out_ref = refs[:3], refs[3]
    for dest in range(4):
        rows = slice(144 * dest, 144 * dest + 144)
        total = first_ref[0, rows].astype(f32)
        for g in got:
            total = total + g[rows].astype(f32)
        out_ref[dest, :144, :] = total.astype(bf16)
    value = first_ref[0, 576:608].astype(f32) + first_ref[0, 608:640].astype(f32)
    for g in got:
        value = value + (g[576:608].astype(f32) + g[608:640].astype(f32))
    hi, lo = pair_split(value)
    for dest in range(4):
        out_ref[dest, 144:176, :] = hi
        out_ref[dest, 176:208, :] = lo


def x_sum(out, got):
    vm = pl.BlockSpec(memory_space=pltpu.VMEM)
    return pl.pallas_call(
        add_kernel,
        grid=(1,),
        in_specs=[pl.BlockSpec((1, 640, 128), lambda i: (0, 0, 0))] + [vm] * 3,
        out_specs=vm,
        out_shape=jax.ShapeDtypeStruct((4, 208, 128), bf16),
        compiler_params=pltpu.CompilerParams(vmem_limit_bytes=6 << 20),
        name="x_sum",
    )(out, *got)


def end_kernel(first_ref, *refs):
    got, (in_ref, out_ref, weight_ref, var_ref, mean_ref) = refs[:3], refs[3:]
    total = first_ref[0].astype(f32)
    for g in got:
        total = total + g[...].astype(f32)
    in_ref[...] = total[:128].T
    out_ref[:, :128] = total[128:136]
    out_ref[:, 128:] = total[136:144]
    value = total[144:176] + total[176:208]
    mean_ref[:, :128] = value[:8]
    mean_ref[:, 128:] = value[16:24]
    weight_ref[...] = value[8, :8]
    var_ref[...] = value[8, 8:16]


def y_sum(out, got):
    vm = pl.BlockSpec(memory_space=pltpu.VMEM)
    return pl.pallas_call(
        end_kernel,
        grid=(1,),
        in_specs=[pl.BlockSpec((1, 208, 128), lambda i: (0, 0, 0))] + [vm] * 3,
        out_specs=[vm] * 5,
        out_shape=[jax.ShapeDtypeStruct((128, 128), f32), jax.ShapeDtypeStruct((8, 256), f32), jax.ShapeDtypeStruct((8,), f32),
                   jax.ShapeDtypeStruct((8,), f32), jax.ShapeDtypeStruct((8, 256), f32)],
        compiler_params=pltpu.CompilerParams(vmem_limit_bytes=6 << 20),
        name="y_sum",
    )(out, *got)


BOTH = ("row", "col")


def device_at(core, x, y, z):
    x, y, z = x % 4, y % 4, z % 4
    return (((y % 2) * 4 + x) * 2 + core) * 8 + z * 2 + y // 2


def shift(v, dx=0, dy=0, dz=0, swap=0):
    pairs = [(device_at(k, x, y, z), device_at(k ^ swap, x + dx, y + dy, z + dz))
             for k in range(2) for x in range(4) for y in range(4) for z in range(4)]
    return lax.ppermute(v, BOTH, sorted(pairs))


def body(series, w_in, w_out, factor_a, factor_b, mix_weight, mix_var, mix_mean):
    row, col = lax.axis_index("row"), lax.axis_index("col")
    core, x, z = lax.rem(row, 2), lax.rem(lax.div(row, 2), 4), lax.div(col, 2)
    y = 2 * lax.rem(col, 2) + lax.div(row, 8)
    at = jnp.stack([core, x, y, z]).astype(jnp.int32)
    pre = jnp.dot(series, w_in, preferred_element_type=f32)
    hidden = jax.nn.silu(pre).astype(bf16)
    emb = jnp.dot(hidden, w_out, preferred_element_type=f32).astype(bf16)
    rowp, colp = prep2(emb, factor_a, factor_b, mix_weight, mix_var, mix_mean)
    near = jnp.concatenate([colp] + [shift(colp, dy=d) for d in (1, 2, 3)], 0)
    near, rowp = lax.optimization_barrier((near, rowp))
    rows = [shift(rowp, dz=d) for d in (1, 2, 3)]
    rows = jnp.concatenate([rowp] + rows, 0)
    rows, series_late = lax.optimization_barrier((rows, series))
    series_z = [series_late] + [shift(series_late, dz=d) for d in (1, 2, 3)]
    rows = jnp.concatenate([rows, shift(rows, swap=1)], 0)
    far = [shift(near, dx=d) for d in (1, 2, 3)]
    far = jnp.concatenate(far, 0)
    inv = 1.0 / (math.pi * mix_var)
    rate, mean_s = rates(mix_var), mix_mean * inv[:, None]
    sums = tile(rate, mean_s, rows, near, final=False)
    rows, far, sums = lax.optimization_barrier((rows, far, sums))
    part, means, v = tile(rate, mean_s, rows, far, prev=sums)
    series_z, part = lax.optimization_barrier((series_z, part))
    half = part.shape[0] // 2
    part = (part[:half] + shift(part[half:], swap=1)).reshape(4, -1, 256)
    part, w_in_late = lax.optimization_barrier((part, w_in))
    grad_embed = part[0]
    for d in (1, 2, 3):
        grad_embed = grad_embed + shift(part[d].astype(bf16), dz=-d).astype(f32)
    emb_cot = grad_embed.astype(bf16)
    small = jnp.concatenate(
        [
            means * inv[:, None],
            jnp.concatenate([0.5 * jnp.sum(v[8:], (1, 2)) / (mix_weight * mix_var * (-2 * math.pi**2)),
                             0.5 / mix_var * jnp.sum(v[:8], (1, 2)), jnp.zeros((240,), f32)])[None],
            jnp.zeros((7, 256), f32),
        ],
        0,
    )
    series_all = series_z + [shift(s, swap=1) for s in series_z]
    hid = w_in.shape[1]
    wide = hid // 4
    k = jnp.arange(hid // 8)
    ids = (2 * (k // 16) + core) * 64 + z * 16 + k % 16
    pick = (jnp.arange(hid)[:, None] == ids[None, :]).astype(bf16)
    w_pick = jnp.dot(w_in_late, pick, preferred_element_type=f32).astype(bf16)
    w_own = lax.dynamic_slice_in_dim(w_in_late, z * wide, wide, 1)
    slope, hid_out = late_pre(w_own, w_pick, series_all)
    sent = jnp.concatenate([emb_cot, *split(small, 2)], 0)
    cots = [sent] + [shift(sent, dz=d) for d in (1, 2, 3)]
    cots, slope, hid_out = lax.optimization_barrier((cots, slope, hid_out))
    cots = cots + [shift(c, swap=1) for c in cots]
    out = late_part(at, slope, hid_out, w_out, cots, series_all)
    out = x_sum(out, [shift(out[d], dx=d) for d in (1, 2, 3)])
    grad_in, grad_out, weights, varies, means = y_sum(out, [shift(out[d], dy=d) for d in (1, 2, 3)])
    return (grad_embed, grad_in, grad_out, weights, varies, means)


def solution(mesh):
    both = P(("row", "col"), None)
    return jax.shard_map(
        body,
        mesh=mesh,
        in_specs=(both, P(), P(), both, both, P(), P(), P()),
        out_specs=(both, P("row", "col"), both, P(), P(), P()),
        check_vma=False,
    )
```

```python
import functools
import math

import jax
import jax.numpy as jnp
import numpy as np
from jax import lax
from jax.experimental import pallas as pl
from jax.experimental.pallas import tpu as pltpu
from jax.sharding import PartitionSpec as P

f32, bf16 = jnp.float32, jnp.bfloat16
NT = (((1,), (1,)), ((), ()))
NN = (((1,), (0,)), ((), ()))


def mm(a, b, dims):
    return lax.dot_general(a, b, dims, preferred_element_type=f32)


def split(x, n):
    out = []
    for _ in range(n):
        h = lax.reduce_precision(x, 8, 7)
        out.append(h.astype(bf16))
        x = x - h
    return out


def rates(mix_var):
    return (-2 * math.pi**2 * math.log2(math.e)) * mix_var


HI = lax.Precision.HIGHEST
TN = (((0,), (0,)), ((), ()))


def sel_matrix():
    m = np.zeros((256, 128), np.float32)
    for q in range(8):
        for t, at in enumerate((64, 72, 88, 96)):
            m[16*(q//4) + 4*t + q%4, at+q] = 1
        m[32+q, 72+q] = 1; m[40+q, 80+q] = 1; m[48+q, 96+q] = 1; m[56+q, 104+q] = 1
    m[64:72, 112:115] = 1
    m[128+115:128+118, :] = 1
    return m


def prep2(emb, fa, fb, mw, mv, mmean):
    ef = emb.astype(f32)
    ang = 2*math.pi*lax.dot_general(ef, mmean, NT, precision=HI)
    c, s = jnp.cos(ang), jnp.sin(ang)
    n = jnp.sum(ef*ef, 1, keepdims=True)
    nh, nm, nl = split(n, 3)
    one = jnp.ones((emb.shape[0], 3), bf16)
    a = mw * (-2*math.pi**2) * mv
    ch, cl = split(c, 2); sh, sl = split(s, 2)
    ah, al = split(c*a, 2); bh, bl = split(s*a, 2)
    z = jnp.zeros((emb.shape[0], 10), bf16)
    colp = jnp.concatenate([emb*-2, fa, fb, ch, cl, ch, sh, sl, sh, nh, nm, nl, one, z], 1)
    rowp = jnp.concatenate([emb, fb, fa, ah, ah, al, bh, bh, bl, one, nh, nm, nl, z], 1)
    return rowp, colp


def tile_kernel(TS, CE2, TR, TC, final, n_prev, rate_ref, sel_ref, mean_ref, row_ref, col_ref, *refs):
    prev, outs = refs[:n_prev], refs[n_prev:]
    if final:
        grad_ref, means_ref, v_ref = outs[:3]
    else:
        pulled_ref, rsum_ref, cs_ref, v_ref = outs[:4]
    outs = outs[3 if final else 4:]
    (rowc_s, d0, d1, o0, o1, m0, m1, c0, c1, pulled_s, rsum_s, cs_s, cst_s, ni_s, nj_s) = outs
    HW = 128
    R, C = row_ref.shape[0], col_ref.shape[0]
    Q = rate_ref.shape[0]
    NC, NR = C // TC, R // TR
    N = NC * NR
    NS = TR // TS
    CW = min(TC, 256)
    lane = lax.broadcasted_iota(jnp.int32, (TS, 128), 1)
    def zero(*refs):
        for r in refs:
            r[...] = jnp.zeros_like(r)
    zero(d0, d1, o0, o1, m0, m1, c0, c1)
    if final:
        zero(means_ref)

    def load_sums(i):
        if prev:
            rows = pl.ds(pl.multiple_of(i * TR, TR), TR)
            pulled_s[...] = prev[0][rows, :]
            rsum_s[...] = prev[1][rows, :]
            cs_s[...] = prev[2][i]
        else:
            zero(pulled_s, rsum_s, cs_s)

    load_sums(0)
    if prev:
        v_ref[...] = prev[3][...]
    else:
        zero(v_ref)
    lr = lax.broadcasted_iota(jnp.int32, (TR, 128), 1)
    sub = lax.broadcasted_iota(jnp.int32, (16, TC), 0)

    def rowcol(t):
        t = jnp.clip(t, 0, N - 1)
        i, j = lax.div(t, NC), lax.rem(t, NC)
        return pl.multiple_of(i * TR, TR), pl.multiple_of(j * TC, TC)

    def products(t, d_s, o_s):
        r0, q0 = rowcol(t)
        cols = pl.ds(q0, TC)
        rows = pl.ds(r0, TR)

        def dist():
            norms = jnp.concatenate([ni_s[rows, :]] * (TC // 128), 1) + nj_s[0:1, cols]
            d_s[...] = norms + mm(row_ref[rows, :256], col_ref[cols, :256], NT)

        def outer():
            rtail = row_ref[rows, 256:384]
            keep = jnp.where((lr < 64) & (t < N), rtail, jnp.zeros_like(rtail))
            o_s[...] = mm(keep, col_ref[cols, 256:384], NT)

        return [dist, outer]

    def sums(t, damp_s, c_s):
        _, q0 = rowcol(t)
        cols = pl.ds(q0, TC)
        acc = [None, None]

        def waves(q):
            r = mm(cst_s[q, :, cols], damp_s[q], NT)
            h = q // 4
            acc[h] = r if acc[h] is None else acc[h] + r
            if q % 4 == 3:
                cs_s[16*h:16*h+16] += acc[h]

        def pull(h):
            M = TR
            rows = slice(h * M, (h + 1) * M)
            emb = col_ref[cols, :256]
            c = c_s[rows, :]
            chi = c.astype(bf16)
            pu = mm(chi, emb, NN)
            if CE2:
                pu = pu + mm((c - chi.astype(f32)).astype(bf16), emb, NN)
            pulled_s[rows, :] += pu
            rs = c[:, :128]
            for k in range(1, TC // 128):
                rs = rs + c[:, k*128:(k+1)*128]
            rsum_s[rows, :] += rs

        return [functools.partial(waves, q) for q in range(Q)], [functools.partial(pull, h) for h in range(1)]

    def stage(t, da, oa, ds, os, ms, cs, mc, cc_):
        first = products(t, da, oa)
        waves, pulls = sums(t - 2, mc, cc_)
        r0, q0 = rowcol(t - 1)
        for s in range(NS):
            rs = slice(s * TS, (s + 1) * TS)
            lhs = rowc_s[pl.ds(pl.multiple_of((r0 + s * TS) * Q, TS * Q), Q*TS), :]
            for cc in range(TC // CW):
                cols = slice(cc*CW, (cc+1)*CW)
                cos = mm(lhs, col_ref[pl.ds(q0 + cc*CW, CW), 256:384], NT)
                for hh in range(CW // HW):
                    sl = slice(hh*HW, (hh+1)*HW)
                    hcols = slice(cc*CW + hh*HW, cc*CW + (hh+1)*HW)
                    d = ds[rs, hcols]
                    o = os[rs, hcols]
                    c = None
                    for q in range(Q):
                        damp = o * jnp.exp2(d * rate_ref[q])
                        ms[q, rs, hcols] = damp.astype(bf16)
                        even = damp * cos[q*TS:(q+1)*TS, sl]
                        c = even if c is None else c + even
                        ed = even * d
                        x = ed[:, :128]
                        for k in range(1, HW // 128):
                            x = x + ed[:, k*128:(k+1)*128]
                        x = x.reshape(TS//8, 8, 128).sum(0)
                        v_ref[q] += x
                        v_ref[Q + q] += even.reshape(TS//8, 8, 128).sum(0)
                    cs[rs, hcols] = c
            for k in range(-(-Q // NS)):
                if waves:
                    waves.pop(0)()
            if s % max(1, NS // 2) == 0 and first:
                first.pop(0)()
            if (s % max(1, NS // 2) == 1 or NS == 2) and pulls:
                pulls.pop(0)()
        for f in first + waves + pulls:
            f()

    def end_rows(t):
        @pl.when((t >= 0) & (lax.rem(t, NC) == NC - 1))
        def _():
            r0, _ = rowcol(t)
            rows = pl.ds(r0, TR)
            if final:
                ef = row_ref[rows, :256].astype(f32)
                cs = cs_s[...]
                wc = jnp.concatenate([cs[0:4] + cs[4:8], cs[16:20] + cs[20:24]], 0)
                ws = jnp.concatenate([cs[8:12] + cs[12:16], cs[24:28] + cs[28:32]], 0)
                rt = mm(sel_ref[32:64], row_ref[rows, 256:384], NT)
                ac = rt[0:8] + rt[8:16]
                as_ = rt[16:24] + rt[24:32]
                spin = as_ * wc - ac * ws
                rowsum = jnp.sum(rsum_s[...], 1, keepdims=True)
                back = lax.dot_general(spin, mean_ref[...], TN, precision=HI, preferred_element_type=f32)
                grad_ref[rows, :] = (2.0 * rowsum * ef + pulled_s[...] + back).astype(grad_ref.dtype)
                means_ref[...] += lax.dot_general(spin, ef, NN, precision=HI, preferred_element_type=f32)
            else:
                pulled_ref[rows, :] = pulled_s[...]
                rsum_ref[rows, :] = rsum_s[...]
                cs_ref[lax.div(t, NC)] = cs_s[...]
            load_sums(jnp.minimum(lax.div(t, NC) + 1, NR - 1))

    for s in range(R // TS):
        x = row_ref[s*TS:(s+1)*TS, 256:384]
        for q in range(Q):
            keep = (lane >= 64) & (lane < 112) & (lane % 8 == q)
            rowc_s[(s*Q+q)*TS:(s*Q+q+1)*TS, :] = jnp.where(keep, x, jnp.zeros_like(x))
    for k in range(C // TC):
        cst = mm(sel_ref[:32], col_ref[k*TC:(k+1)*TC, 256:384], NT)
        for q in range(Q):
            keep = cst[16*(q//4):16*(q//4)+16]
            cst_s[q, :, k*TC:(k+1)*TC] = jnp.where(sub % 4 == q % 4, keep, 0.0).astype(bf16)
        nj_s[:, k*TC:(k+1)*TC] = mm(sel_ref[64:72], col_ref[k*TC:(k+1)*TC, 256:384], NT)
    for k in range(R // TR):
        ni_s[k*TR:(k+1)*TR, :] = mm(row_ref[k*TR:(k+1)*TR, 256:384], sel_ref[128:256], NN)

    def pair(h, _):
        t = 2 * h
        stage(t, d0, o0, d1, o1, m1, c1, m0, c0)
        stage(t + 1, d1, o1, d0, o0, m0, c0, m1, c1)
        end_rows(t - 1)
        return 0
    lax.fori_loop(0, (N + 2) // 2, pair, 0)

def tile(rate, mean_s, rowp, colp, prev=(), final=True, TR=256, TC=256, TS=64, CE2=False):
    R, C, Q = rowp.shape[0], colp.shape[0], rate.shape[0]
    assert (R // TR) * (C // TC) % 2 == 0
    vm = pl.BlockSpec(memory_space=pltpu.VMEM)
    sc = lambda *s: pltpu.VMEM(s, f32)
    shape = lambda *dims: jax.ShapeDtypeStruct(dims, f32)
    if final:
        shapes = [shape(R, 256), shape(8, 256), shape(2 * Q, 8, 128)]
    else:
        shapes = [shape(R, 256), shape(R, 128), shape(R // TR, 32, TR), shape(2 * Q, 8, 128)]
    return pl.pallas_call(
        functools.partial(tile_kernel, TS, CE2, TR, TC, final, len(prev)),
        in_specs=[pl.BlockSpec(memory_space=pltpu.SMEM), vm, vm, vm, vm] + [vm] * len(prev),
        out_specs=[vm] * len(shapes),
        out_shape=shapes,
        scratch_shapes=[pltpu.VMEM((R*Q, 128), bf16), sc(TR, TC), sc(TR, TC), sc(TR, TC), sc(TR, TC),
                        pltpu.VMEM((Q, TR, TC), bf16), pltpu.VMEM((Q, TR, TC), bf16), sc(TR, TC), sc(TR, TC),
                        sc(TR, 256), sc(TR, 128), sc(32, TR), pltpu.VMEM((Q, 16, C), bf16), sc(R, 128), sc(8, C)],
        cost_estimate=pl.CostEstimate(flops=20 * R * C * 256, bytes_accessed=4 * 10**6, transcendentals=R * C * Q),
        compiler_params=pltpu.CompilerParams(vmem_limit_bytes=20 << 20),
        name="tile",
    )(rate, jnp.asarray(sel_matrix(), bf16), mean_s, rowp, colp, *prev)


def pre_kernel(w_ref, wh_ref, *refs):
    pieces, (slope_ref, hid_ref) = refs[:-2], refs[-2:]
    for p in range(0, len(pieces), 2):
        two = jnp.concatenate([pieces[p][...], pieces[p+1][...]], 0)
        n = two.shape[0]
        cols = slice(p * n // 2, (p + 2) * n // 2)
        pre = mm(two, w_ref[...], NN)
        sig = jax.nn.sigmoid(pre)
        slope_ref[:, cols] = (sig * (1.0 + pre * (1.0 - sig))).T
        pre = mm(two, wh_ref[...], NN)
        hid_ref[:, cols] = (pre * jax.nn.sigmoid(pre)).T.astype(bf16)


def late_pre(w_own, w_pick, pieces):
    vm = pl.BlockSpec(memory_space=pltpu.VMEM)
    tok = sum(p.shape[0] for p in pieces)
    return pl.pallas_call(
        pre_kernel,
        in_specs=[vm] * (2 + len(pieces)),
        out_specs=[vm, vm],
        out_shape=[jax.ShapeDtypeStruct((w_own.shape[1], tok), f32), jax.ShapeDtypeStruct((w_pick.shape[1], tok), bf16)],
        cost_estimate=pl.CostEstimate(flops=4 * 10**9, bytes_accessed=6 * 10**6, transcendentals=400000),
        compiler_params=pltpu.CompilerParams(vmem_limit_bytes=20 << 20),
        name="pre",
    )(w_own, w_pick, *pieces)


def pair_split(x):
    h = x.astype(bf16)
    return h, (x - h.astype(f32)).astype(bf16)


def part_kernel(own, n, at_ref, slope_ref, hid_ref, w_ref, *refs):
    cots, pieces, (out_ref,) = refs[:n], refs[n:2*n], refs[2*n:]
    core, x, y, z = at_ref[0], at_ref[1], at_ref[2], at_ref[3]
    wide = slope_ref.shape[0]
    cot = jnp.concatenate([c[:own, :] for c in cots], 0)
    small = cots[0][own:own+16, :].astype(f32) + cots[0][own+16:own+32, :].astype(f32)
    for c in cots[1:]:
        small = small + (c[own:own+16, :].astype(f32) + c[own+16:own+32, :].astype(f32))
    hi, lo = pair_split(small)
    for k, part in enumerate((hi, lo)):
        for dest in range(4):
            out_ref[dest, 576+32*k:592+32*k, :] = part[:, :128]
            out_ref[dest, 592+32*k:608+32*k, :] = part[:, 128:]
    back = mm(w_ref[pl.ds(pl.multiple_of(z * wide, wide), wide), :], cot, NT)
    d = (back * slope_ref[...]).astype(bf16)
    grad_out = mm(hid_ref[...], cot, NN)
    for m in range(8):
        feats = pl.ds(pl.multiple_of((2 * m + core) * 128, 128), 128)
        g = mm(d, jnp.concatenate([p[:, feats] for p in pieces], 0), NN)
        sx = lax.rem(m % 4 - x + 4, 4)
        for h in range(2):
            sy = lax.rem(2 * h + m // 4 - y + 4, 4)
            base = pl.multiple_of(sy * 144, 16)
            out_ref[sx, pl.ds(base, 128), :] = g[h*128:(h+1)*128].astype(bf16)
            o = grad_out[16*m+8*h:16*m+8*h+8]
            out_ref[sx, pl.ds(base + 128, 16), :] = jnp.concatenate([o[:, :128], o[:, 128:]], 0).astype(bf16)


def late_part(at, slope, hid_out, w_out, cots, pieces):
    vm = pl.BlockSpec(memory_space=pltpu.VMEM)
    n = len(pieces)
    return pl.pallas_call(
        functools.partial(part_kernel, pieces[0].shape[0], n),
        in_specs=[pl.BlockSpec(memory_space=pltpu.SMEM)] + [vm] * (3 + 2 * n),
        out_specs=vm,
        out_shape=jax.ShapeDtypeStruct((4, 640, 128), bf16),
        cost_estimate=pl.CostEstimate(flops=2 * 10**9, bytes_accessed=6 * 10**6, transcendentals=0),
        compiler_params=pltpu.CompilerParams(vmem_limit_bytes=20 << 20),
        name="part",
    )(at, slope, hid_out, w_out, *cots, *pieces)


def add_kernel(first_ref, *refs):
    got, out_ref = refs[:3], refs[3]
    for dest in range(4):
        rows = slice(144 * dest, 144 * dest + 144)
        total = first_ref[0, rows].astype(f32)
        for g in got:
            total = total + g[rows].astype(f32)
        out_ref[dest, :144, :] = total.astype(bf16)
    value = first_ref[0, 576:608].astype(f32) + first_ref[0, 608:640].astype(f32)
    for g in got:
        value = value + (g[576:608].astype(f32) + g[608:640].astype(f32))
    hi, lo = pair_split(value)
    for dest in range(4):
        out_ref[dest, 144:176, :] = hi
        out_ref[dest, 176:208, :] = lo


def x_sum(out, got):
    vm = pl.BlockSpec(memory_space=pltpu.VMEM)
    return pl.pallas_call(
        add_kernel,
        grid=(1,),
        in_specs=[pl.BlockSpec((1, 640, 128), lambda i: (0, 0, 0))] + [vm] * 3,
        out_specs=vm,
        out_shape=jax.ShapeDtypeStruct((4, 208, 128), bf16),
        compiler_params=pltpu.CompilerParams(vmem_limit_bytes=6 << 20),
        name="x_sum",
    )(out, *got)


def end_kernel(first_ref, *refs):
    got, (in_ref, out_ref, weight_ref, var_ref, mean_ref) = refs[:3], refs[3:]
    total = first_ref[0].astype(f32)
    for g in got:
        total = total + g[...].astype(f32)
    in_ref[...] = total[:128].T
    out_ref[:, :128] = total[128:136]
    out_ref[:, 128:] = total[136:144]
    value = total[144:176] + total[176:208]
    mean_ref[:, :128] = value[:8]
    mean_ref[:, 128:] = value[16:24]
    weight_ref[...] = value[8, :8]
    var_ref[...] = value[8, 8:16]


def y_sum(out, got):
    vm = pl.BlockSpec(memory_space=pltpu.VMEM)
    return pl.pallas_call(
        end_kernel,
        grid=(1,),
        in_specs=[pl.BlockSpec((1, 208, 128), lambda i: (0, 0, 0))] + [vm] * 3,
        out_specs=[vm] * 5,
        out_shape=[jax.ShapeDtypeStruct((128, 128), f32), jax.ShapeDtypeStruct((8, 256), f32), jax.ShapeDtypeStruct((8,), f32),
                   jax.ShapeDtypeStruct((8,), f32), jax.ShapeDtypeStruct((8, 256), f32)],
        compiler_params=pltpu.CompilerParams(vmem_limit_bytes=6 << 20),
        name="y_sum",
    )(out, *got)


BOTH = ("row", "col")


def device_at(core, x, y, z):
    x, y, z = x % 4, y % 4, z % 4
    return (((y % 2) * 4 + x) * 2 + core) * 8 + z * 2 + y // 2


def shift(v, dx=0, dy=0, dz=0, swap=0):
    pairs = [(device_at(k, x, y, z), device_at(k ^ swap, x + dx, y + dy, z + dz))
             for k in range(2) for x in range(4) for y in range(4) for z in range(4)]
    return lax.ppermute(v, BOTH, sorted(pairs))


def body(series, w_in, w_out, factor_a, factor_b, mix_weight, mix_var, mix_mean):
    row, col = lax.axis_index("row"), lax.axis_index("col")
    core, x, z = lax.rem(row, 2), lax.rem(lax.div(row, 2), 4), lax.div(col, 2)
    y = 2 * lax.rem(col, 2) + lax.div(row, 8)
    at = jnp.stack([core, x, y, z]).astype(jnp.int32)
    pre = jnp.dot(series, w_in, preferred_element_type=f32)
    hidden = jax.nn.silu(pre).astype(bf16)
    emb = jnp.dot(hidden, w_out, preferred_element_type=f32).astype(bf16)
    rowp, colp = prep2(emb, factor_a, factor_b, mix_weight, mix_var, mix_mean)
    rows = jnp.concatenate([rowp] + [shift(rowp, dz=d) for d in (1, 2, 3)], 0)
    rows, series_late = lax.optimization_barrier((rows, series))
    series_z = [series_late] + [shift(series_late, dz=d) for d in (1, 2, 3)]
    near = jnp.concatenate([colp] + [shift(colp, dy=d) for d in (1, 2, 3)], 0)
    rows = jnp.concatenate([rows, shift(rows, swap=1)], 0)
    near, w_in_late = lax.optimization_barrier((near, w_in))
    far = jnp.concatenate([shift(near, dx=d) for d in (1, 2, 3)], 0)
    inv = 1.0 / (math.pi * mix_var)
    rate, mean_s = rates(mix_var), mix_mean * inv[:, None]
    sums = tile(rate, mean_s, rows, near, final=False)
    hid = w_in.shape[1]
    wide = hid // 4
    k = jnp.arange(hid // 8)
    ids = (2 * (k // 16) + core) * 64 + z * 16 + k % 16
    pick = (jnp.arange(hid)[:, None] == ids[None, :]).astype(bf16)
    w_pick = jnp.dot(w_in_late, pick, preferred_element_type=f32).astype(bf16)
    w_own = lax.dynamic_slice_in_dim(w_in_late, z * wide, wide, 1)
    rows, far, sums, w_own, w_pick = lax.optimization_barrier((rows, far, sums, w_own, w_pick))
    part, means, v = tile(rate, mean_s, rows, far, prev=sums)
    series_z, part = lax.optimization_barrier((series_z, part))
    half = part.shape[0] // 2
    part = (part[:half] + shift(part[half:], swap=1)).reshape(4, -1, 256)
    grad_embed = part[0]
    for d in (1, 2, 3):
        grad_embed = grad_embed + shift(part[d].astype(bf16), dz=-d).astype(f32)
    emb_cot = grad_embed.astype(bf16)
    small = jnp.concatenate(
        [
            means * inv[:, None],
            jnp.concatenate([0.5 * jnp.sum(v[8:], (1, 2)) / (mix_weight * mix_var * (-2 * math.pi**2)),
                             0.5 / mix_var * jnp.sum(v[:8], (1, 2)), jnp.zeros((240,), f32)])[None],
            jnp.zeros((7, 256), f32),
        ],
        0,
    )
    series_all = series_z + [shift(s, swap=1) for s in series_z]
    slope, hid_out = late_pre(w_own, w_pick, series_all)
    sent = jnp.concatenate([emb_cot, *split(small, 2)], 0)
    cots = [sent] + [shift(sent, dz=d) for d in (1, 2, 3)]
    cots, slope, hid_out = lax.optimization_barrier((cots, slope, hid_out))
    cots = cots + [shift(c, swap=1) for c in cots]
    out = late_part(at, slope, hid_out, w_out, cots, series_all)
    out = x_sum(out, [shift(out[d], dx=d) for d in (1, 2, 3)])
    grad_in, grad_out, weights, varies, means = y_sum(out, [shift(out[d], dy=d) for d in (1, 2, 3)])
    return (grad_embed, grad_in, grad_out, weights, varies, means)


def solution(mesh):
    both = P(("row", "col"), None)
    return jax.shard_map(
        body,
        mesh=mesh,
        in_specs=(both, P(), P(), both, both, P(), P(), P()),
        out_specs=(both, P("row", "col"), both, P(), P(), P()),
        check_vma=False,
    )
```

```python
import functools
import math

import jax
import jax.numpy as jnp
import numpy as np
from jax import lax
from jax.experimental import pallas as pl
from jax.experimental.pallas import tpu as pltpu
from jax.sharding import PartitionSpec as P

f32, bf16 = jnp.float32, jnp.bfloat16
NT = (((1,), (1,)), ((), ()))
NN = (((1,), (0,)), ((), ()))


def mm(a, b, dims):
    return lax.dot_general(a, b, dims, preferred_element_type=f32)


def split(x, n):
    out = []
    for _ in range(n):
        h = lax.reduce_precision(x, 8, 7)
        out.append(h.astype(bf16))
        x = x - h
    return out


def rates(mix_var):
    return (-2 * math.pi**2 * math.log2(math.e)) * mix_var


HI = lax.Precision.HIGHEST
TN = (((0,), (0,)), ((), ()))


def sel_matrix():
    m = np.zeros((256, 128), np.float32)
    for q in range(8):
        for t, at in enumerate((64, 72, 88, 96)):
            m[16*(q//4) + 4*t + q%4, at+q] = 1
        m[32+q, 72+q] = 1; m[40+q, 80+q] = 1; m[48+q, 96+q] = 1; m[56+q, 104+q] = 1
    m[64:72, 112:115] = 1
    m[128+115:128+118, :] = 1
    return m


def prep2(emb, fa, fb, mw, mv, mmean):
    ef = emb.astype(f32)
    ang = 2*math.pi*lax.dot_general(ef, mmean, NT, precision=HI)
    c, s = jnp.cos(ang), jnp.sin(ang)
    n = jnp.sum(ef*ef, 1, keepdims=True)
    nh, nm, nl = split(n, 3)
    one = jnp.ones((emb.shape[0], 3), bf16)
    a = mw * (-2*math.pi**2) * mv
    ch, cl = split(c, 2); sh, sl = split(s, 2)
    ah, al = split(c*a, 2); bh, bl = split(s*a, 2)
    z = jnp.zeros((emb.shape[0], 10), bf16)
    colp = jnp.concatenate([emb*-2, fa, fb, ch, cl, ch, sh, sl, sh, nh, nm, nl, one, z], 1)
    rowp = jnp.concatenate([emb, fb, fa, ah, ah, al, bh, bh, bl, one, nh, nm, nl, z], 1)
    return rowp, colp


def halves(x):
    one = x.astype(bf16).astype(f32)
    return one, (x - one).astype(bf16).astype(f32)


def tile_kernel(TS, CE2, TR, TC, final, n_prev, rate_ref, sel_ref, mean_ref, row_ref, col_ref, *refs):
    prev, outs = refs[:n_prev], refs[n_prev:]
    if final:
        grad_ref, means_ref, v_ref = outs[:3]
    else:
        pulled_ref, rsum_ref, cs_ref, v_ref, rowc_s = outs[:5]
    outs = outs[3 if final else 5:]
    if prev:
        rowc_s = prev[4]
    elif final:
        rowc_s, outs = outs[0], outs[1:]
    (d0, d1, o0, o1, m0, m1, c0, c1, pulled_s, rsum_s, cs_s, cst_s, ni_s, nj_s) = outs
    HW = 128
    R, C = row_ref.shape[0], col_ref.shape[0]
    Q = rate_ref.shape[0]
    NC, NR = C // TC, R // TR
    N = NC * NR
    NS = TR // TS
    CW = min(TC, 256)
    lane = lax.broadcasted_iota(jnp.int32, (TS, 128), 1)
    def zero(*refs):
        for r in refs:
            r[...] = jnp.zeros_like(r)
    zero(d1, o1, m0, c0)
    if final:
        zero(means_ref)

    def load_sums(i):
        if prev:
            rows = pl.ds(pl.multiple_of(i * TR, TR), TR)
            pulled_s[...] = prev[0][rows, :]
            rsum_s[...] = prev[1][rows, :]
            cs_s[...] = prev[2][i]
        else:
            zero(pulled_s, rsum_s, cs_s)

    load_sums(0)
    if prev:
        v_ref[...] = prev[3][...]
    else:
        zero(v_ref)
    lr = lax.broadcasted_iota(jnp.int32, (TR, 128), 1)
    sub = lax.broadcasted_iota(jnp.int32, (16, TC), 0)

    def rowcol(t):
        t = jnp.clip(t, 0, N - 1)
        i, j = lax.div(t, NC), lax.rem(t, NC)
        return pl.multiple_of(i * TR, TR), pl.multiple_of(j * TC, TC)

    def products(t, d_s, o_s):
        r0, q0 = rowcol(t)
        cols = pl.ds(q0, TC)
        rows = pl.ds(r0, TR)

        def dist():
            norms = jnp.concatenate([ni_s[rows, :]] * (TC // 128), 1) + nj_s[0:1, cols]
            d_s[...] = norms + mm(row_ref[rows, :256], col_ref[cols, :256], NT)

        def outer():
            rtail = row_ref[rows, 256:384]
            keep = jnp.where((lr < 64) & (t < N), rtail, jnp.zeros_like(rtail))
            o_s[...] = mm(keep, col_ref[cols, 256:384], NT)

        return [dist, outer]

    def sums(t, damp_s, c_s):
        _, q0 = rowcol(t)
        cols = pl.ds(q0, TC)
        acc = [None, None]

        def waves(q):
            r = mm(cst_s[q, :, cols], damp_s[q], NT)
            h = q // 4
            acc[h] = r if acc[h] is None else acc[h] + r
            if q % 4 == 3:
                cs_s[16*h:16*h+16] += acc[h]

        def pull(h):
            M = TR
            rows = slice(h * M, (h + 1) * M)
            emb = col_ref[cols, :256]
            c = c_s[rows, :]
            chi = c.astype(bf16)
            pu = mm(chi, emb, NN)
            if CE2:
                pu = pu + mm((c - chi.astype(f32)).astype(bf16), emb, NN)
            pulled_s[rows, :] += pu
            rs = c[:, :128]
            for k in range(1, TC // 128):
                rs = rs + c[:, k*128:(k+1)*128]
            rsum_s[rows, :] += rs

        return [functools.partial(waves, q) for q in range(Q)], [functools.partial(pull, h) for h in range(1)]

    def stage(t, da, oa, ds, os, ms, cs, mc, cc_):
        first = products(t, da, oa)
        waves, pulls = sums(t - 2, mc, cc_)
        r0, q0 = rowcol(t - 1)
        for s in range(NS):
            rs = slice(s * TS, (s + 1) * TS)
            lhs = rowc_s[pl.ds(pl.multiple_of((r0 + s * TS) * Q, TS * Q), Q*TS), :]
            for cc in range(TC // CW):
                cols = slice(cc*CW, (cc+1)*CW)
                cos = mm(lhs, col_ref[pl.ds(q0 + cc*CW, CW), 256:384], NT)
                for hh in range(CW // HW):
                    sl = slice(hh*HW, (hh+1)*HW)
                    hcols = slice(cc*CW + hh*HW, cc*CW + (hh+1)*HW)
                    d = ds[rs, hcols]
                    o = os[rs, hcols]
                    c = None
                    for q in range(Q):
                        damp = o * jnp.exp2(d * rate_ref[q])
                        ms[q, rs, hcols] = damp.astype(bf16)
                        even = damp * cos[q*TS:(q+1)*TS, sl]
                        c = even if c is None else c + even
                        ed = even * d
                        x = ed[:, :128]
                        for k in range(1, HW // 128):
                            x = x + ed[:, k*128:(k+1)*128]
                        x = x.reshape(TS//8, 8, 128).sum(0)
                        v_ref[q] += x
                        v_ref[Q + q] += even.reshape(TS//8, 8, 128).sum(0)
                    cs[rs, hcols] = c
            for k in range(-(-Q // NS)):
                if waves:
                    waves.pop(0)()
            if s % max(1, NS // 2) == 0 and first:
                first.pop(0)()
            if (s % max(1, NS // 2) == 1 or NS == 2) and pulls:
                pulls.pop(0)()
        for f in first + waves + pulls:
            f()

    def end_rows(t):
        @pl.when((t >= 0) & (lax.rem(t, NC) == NC - 1))
        def _():
            r0, _ = rowcol(t)
            rows = pl.ds(r0, TR)
            if final:
                ef = row_ref[rows, :256].astype(f32)
                cs = cs_s[...]
                wc = jnp.concatenate([cs[0:4] + cs[4:8], cs[16:20] + cs[20:24]], 0)
                ws = jnp.concatenate([cs[8:12] + cs[12:16], cs[24:28] + cs[28:32]], 0)
                rt = mm(sel_ref[32:64], row_ref[rows, 256:384], NT)
                ac = rt[0:8] + rt[8:16]
                as_ = rt[16:24] + rt[24:32]
                spin = as_ * wc - ac * ws
                rowsum = jnp.sum(rsum_s[...], 1, keepdims=True)
                one, two = halves(spin)
                m_one, m_two = halves(mean_ref[...])
                pad = jnp.zeros_like(one)
                back = mm(jnp.concatenate([one, two, one, pad], 0).astype(bf16),
                          jnp.concatenate([m_one, m_one, m_two, jnp.zeros_like(m_one)], 0).astype(bf16), TN)
                grad_ref[rows, :] = (2.0 * rowsum * ef + pulled_s[...] + back).astype(grad_ref.dtype)
                both = mm(jnp.concatenate([one, two], 0).astype(bf16), row_ref[rows, :256], NN)
                means_ref[...] += both[:8] + both[8:]
            else:
                pulled_ref[rows, :] = pulled_s[...]
                rsum_ref[rows, :] = rsum_s[...]
                cs_ref[lax.div(t, NC)] = cs_s[...]
            load_sums(jnp.minimum(lax.div(t, NC) + 1, NR - 1))

    if not prev:
        for s in range(R // TS):
            x = row_ref[s*TS:(s+1)*TS, 256:384]
            for q in range(Q):
                keep = (lane >= 64) & (lane < 112) & (lane % 8 == q)
                rowc_s[(s*Q+q)*TS:(s*Q+q+1)*TS, :] = jnp.where(keep, x, jnp.zeros_like(x))
    for k in range(C // TC):
        cst = mm(sel_ref[:32], col_ref[k*TC:(k+1)*TC, 256:384], NT)
        for q in range(Q):
            keep = cst[16*(q//4):16*(q//4)+16]
            cst_s[q, :, k*TC:(k+1)*TC] = jnp.where(sub % 4 == q % 4, keep, 0.0).astype(bf16)
        nj_s[:, k*TC:(k+1)*TC] = mm(sel_ref[64:72], col_ref[k*TC:(k+1)*TC, 256:384], NT)
    for k in range(R // TR):
        ni_s[k*TR:(k+1)*TR, :] = mm(row_ref[k*TR:(k+1)*TR, 256:384], sel_ref[128:256], NN)

    def pair(h, _):
        t = 2 * h
        stage(t, d0, o0, d1, o1, m1, c1, m0, c0)
        stage(t + 1, d1, o1, d0, o0, m0, c0, m1, c1)
        end_rows(t - 1)
        return 0
    lax.fori_loop(0, (N + 2) // 2, pair, 0)

def tile(rate, mean_s, rowp, colp, prev=(), final=True, TR=256, TC=256, TS=64, CE2=False):
    R, C, Q = rowp.shape[0], colp.shape[0], rate.shape[0]
    assert (R // TR) * (C // TC) % 2 == 0
    vm = pl.BlockSpec(memory_space=pltpu.VMEM)
    sc = lambda *s: pltpu.VMEM(s, f32)
    shape = lambda *dims: jax.ShapeDtypeStruct(dims, f32)
    if final:
        shapes = [shape(R, 256), shape(8, 256), shape(2 * Q, 8, 128)]
    else:
        shapes = [shape(R, 256), shape(R, 128), shape(R // TR, 32, TR), shape(2 * Q, 8, 128),
                  jax.ShapeDtypeStruct((R * Q, 128), bf16)]
    return pl.pallas_call(
        functools.partial(tile_kernel, TS, CE2, TR, TC, final, len(prev)),
        in_specs=[pl.BlockSpec(memory_space=pltpu.SMEM), vm, vm, vm, vm] + [vm] * len(prev),
        out_specs=[vm] * len(shapes),
        out_shape=shapes,
        scratch_shapes=([pltpu.VMEM((R*Q, 128), bf16)] if final and not prev else []) + [sc(TR, TC), sc(TR, TC), sc(TR, TC), sc(TR, TC),
                        pltpu.VMEM((Q, TR, TC), bf16), pltpu.VMEM((Q, TR, TC), bf16), sc(TR, TC), sc(TR, TC),
                        sc(TR, 256), sc(TR, 128), sc(32, TR), pltpu.VMEM((Q, 16, C), bf16), sc(R, 128), sc(8, C)],
        cost_estimate=pl.CostEstimate(flops=20 * R * C * 256, bytes_accessed=4 * 10**6, transcendentals=R * C * Q),
        compiler_params=pltpu.CompilerParams(vmem_limit_bytes=20 << 20),
        name="tile",
    )(rate, jnp.asarray(sel_matrix(), bf16), mean_s, rowp, colp, *prev)


def pre_kernel(w_ref, wh_ref, *refs):
    pieces, (slope_ref, hid_ref) = refs[:-2], refs[-2:]
    for p in range(0, len(pieces), 2):
        two = jnp.concatenate([pieces[p][...], pieces[p+1][...]], 0)
        n = two.shape[0]
        cols = slice(p * n // 2, (p + 2) * n // 2)
        pre = mm(two, w_ref[...], NN)
        sig = jax.nn.sigmoid(pre)
        slope_ref[:, cols] = (sig * (1.0 + pre * (1.0 - sig))).T
        pre = mm(two, wh_ref[...], NN)
        hid_ref[:, cols] = (pre * jax.nn.sigmoid(pre)).T.astype(bf16)


def late_pre(w_own, w_pick, pieces):
    vm = pl.BlockSpec(memory_space=pltpu.VMEM)
    tok = sum(p.shape[0] for p in pieces)
    return pl.pallas_call(
        pre_kernel,
        in_specs=[vm] * (2 + len(pieces)),
        out_specs=[vm, vm],
        out_shape=[jax.ShapeDtypeStruct((w_own.shape[1], tok), f32), jax.ShapeDtypeStruct((w_pick.shape[1], tok), bf16)],
        cost_estimate=pl.CostEstimate(flops=4 * 10**9, bytes_accessed=6 * 10**6, transcendentals=400000),
        compiler_params=pltpu.CompilerParams(vmem_limit_bytes=20 << 20),
        name="pre",
    )(w_own, w_pick, *pieces)


def pair_split(x):
    h = x.astype(bf16)
    return h, (x - h.astype(f32)).astype(bf16)


def part_kernel(own, n, at_ref, slope_ref, hid_ref, w_ref, *refs):
    cots, pieces, (out_ref,) = refs[:n], refs[n:2*n], refs[2*n:]
    core, x, y, z = at_ref[0], at_ref[1], at_ref[2], at_ref[3]
    wide = slope_ref.shape[0]
    cot = jnp.concatenate([c[:own, :] for c in cots], 0)
    small = cots[0][own:own+16, :].astype(f32) + cots[0][own+16:own+32, :].astype(f32)
    for c in cots[1:]:
        small = small + (c[own:own+16, :].astype(f32) + c[own+16:own+32, :].astype(f32))
    hi, lo = pair_split(small)
    for k, part in enumerate((hi, lo)):
        for dest in range(4):
            out_ref[dest, 576+32*k:592+32*k, :] = part[:, :128]
            out_ref[dest, 592+32*k:608+32*k, :] = part[:, 128:]
    back = mm(w_ref[pl.ds(pl.multiple_of(z * wide, wide), wide), :], cot, NT)
    d = (back * slope_ref[...]).astype(bf16)
    grad_out = mm(hid_ref[...], cot, NN)
    for m in range(8):
        feats = pl.ds(pl.multiple_of((2 * m + core) * 128, 128), 128)
        g = mm(d, jnp.concatenate([p[:, feats] for p in pieces], 0), NN)
        sx = lax.rem(m % 4 - x + 4, 4)
        for h in range(2):
            sy = lax.rem(2 * h + m // 4 - y + 4, 4)
            base = pl.multiple_of(sy * 144, 16)
            out_ref[sx, pl.ds(base, 128), :] = g[h*128:(h+1)*128].astype(bf16)
            o = grad_out[16*m+8*h:16*m+8*h+8]
            out_ref[sx, pl.ds(base + 128, 16), :] = jnp.concatenate([o[:, :128], o[:, 128:]], 0).astype(bf16)


def late_part(at, slope, hid_out, w_out, cots, pieces):
    vm = pl.BlockSpec(memory_space=pltpu.VMEM)
    n = len(pieces)
    return pl.pallas_call(
        functools.partial(part_kernel, pieces[0].shape[0], n),
        in_specs=[pl.BlockSpec(memory_space=pltpu.SMEM)] + [vm] * (3 + 2 * n),
        out_specs=vm,
        out_shape=jax.ShapeDtypeStruct((4, 640, 128), bf16),
        cost_estimate=pl.CostEstimate(flops=2 * 10**9, bytes_accessed=6 * 10**6, transcendentals=0),
        compiler_params=pltpu.CompilerParams(vmem_limit_bytes=20 << 20),
        name="part",
    )(at, slope, hid_out, w_out, *cots, *pieces)


def add_kernel(first_ref, *refs):
    got, out_ref = refs[:3], refs[3]
    for dest in range(4):
        rows = slice(144 * dest, 144 * dest + 144)
        total = first_ref[0, rows].astype(f32)
        for g in got:
            total = total + g[rows].astype(f32)
        out_ref[dest, :144, :] = total.astype(bf16)
    value = first_ref[0, 576:608].astype(f32) + first_ref[0, 608:640].astype(f32)
    for g in got:
        value = value + (g[576:608].astype(f32) + g[608:640].astype(f32))
    hi, lo = pair_split(value)
    for dest in range(4):
        out_ref[dest, 144:176, :] = hi
        out_ref[dest, 176:208, :] = lo


def x_sum(out, got):
    vm = pl.BlockSpec(memory_space=pltpu.VMEM)
    return pl.pallas_call(
        add_kernel,
        grid=(1,),
        in_specs=[pl.BlockSpec((1, 640, 128), lambda i: (0, 0, 0))] + [vm] * 3,
        out_specs=vm,
        out_shape=jax.ShapeDtypeStruct((4, 208, 128), bf16),
        compiler_params=pltpu.CompilerParams(vmem_limit_bytes=6 << 20),
        name="x_sum",
    )(out, *got)


def end_kernel(first_ref, *refs):
    got, (in_ref, out_ref, weight_ref, var_ref, mean_ref) = refs[:3], refs[3:]
    total = first_ref[0].astype(f32)
    for g in got:
        total = total + g[...].astype(f32)
    in_ref[...] = total[:128].T
    out_ref[:, :128] = total[128:136]
    out_ref[:, 128:] = total[136:144]
    value = total[144:176] + total[176:208]
    mean_ref[:, :128] = value[:8]
    mean_ref[:, 128:] = value[16:24]
    weight_ref[...] = value[8, :8]
    var_ref[...] = value[8, 8:16]


def y_sum(out, got):
    vm = pl.BlockSpec(memory_space=pltpu.VMEM)
    return pl.pallas_call(
        end_kernel,
        grid=(1,),
        in_specs=[pl.BlockSpec((1, 208, 128), lambda i: (0, 0, 0))] + [vm] * 3,
        out_specs=[vm] * 5,
        out_shape=[jax.ShapeDtypeStruct((128, 128), f32), jax.ShapeDtypeStruct((8, 256), f32), jax.ShapeDtypeStruct((8,), f32),
                   jax.ShapeDtypeStruct((8,), f32), jax.ShapeDtypeStruct((8, 256), f32)],
        compiler_params=pltpu.CompilerParams(vmem_limit_bytes=6 << 20),
        name="y_sum",
    )(out, *got)


BOTH = ("row", "col")


def device_at(core, x, y, z):
    x, y, z = x % 4, y % 4, z % 4
    return (((y % 2) * 4 + x) * 2 + core) * 8 + z * 2 + y // 2


def shift(v, dx=0, dy=0, dz=0, swap=0):
    pairs = [(device_at(k, x, y, z), device_at(k ^ swap, x + dx, y + dy, z + dz))
             for k in range(2) for x in range(4) for y in range(4) for z in range(4)]
    return lax.ppermute(v, BOTH, sorted(pairs))


def body(series, w_in, w_out, factor_a, factor_b, mix_weight, mix_var, mix_mean):
    row, col = lax.axis_index("row"), lax.axis_index("col")
    core, x, z = lax.rem(row, 2), lax.rem(lax.div(row, 2), 4), lax.div(col, 2)
    y = 2 * lax.rem(col, 2) + lax.div(row, 8)
    at = jnp.stack([core, x, y, z]).astype(jnp.int32)
    pre = jnp.dot(series, w_in, preferred_element_type=f32)
    hidden = jax.nn.silu(pre).astype(bf16)
    emb = jnp.dot(hidden, w_out, preferred_element_type=f32).astype(bf16)
    rowp, colp = prep2(emb, factor_a, factor_b, mix_weight, mix_var, mix_mean)
    rows = jnp.concatenate([rowp] + [shift(rowp, dz=d) for d in (1, 2, 3)], 0)
    rows, series_late = lax.optimization_barrier((rows, series))
    series_z = [series_late] + [shift(series_late, dz=d) for d in (1, 2, 3)]
    near = jnp.concatenate([colp] + [shift(colp, dy=d) for d in (1, 2, 3)], 0)
    rows = jnp.concatenate([rows, shift(rows, swap=1)], 0)
    near, w_in_late = lax.optimization_barrier((near, w_in))
    far = jnp.concatenate([shift(near, dx=d) for d in (1, 2, 3)], 0)
    inv = 1.0 / (math.pi * mix_var)
    rate, mean_s = rates(mix_var), mix_mean * inv[:, None]
    sums = tile(rate, mean_s, rows, near, final=False)
    hid = w_in.shape[1]
    wide = hid // 4
    k = jnp.arange(hid // 8)
    ids = (2 * (k // 16) + core) * 64 + z * 16 + k % 16
    pick = (jnp.arange(hid)[:, None] == ids[None, :]).astype(bf16)
    w_pick = jnp.dot(w_in_late, pick, preferred_element_type=f32).astype(bf16)
    w_own = lax.dynamic_slice_in_dim(w_in_late, z * wide, wide, 1)
    rows, far, sums, w_own, w_pick = lax.optimization_barrier((rows, far, sums, w_own, w_pick))
    part, means, v = tile(rate, mean_s, rows, far, prev=sums)
    series_z, part = lax.optimization_barrier((series_z, part))
    half = part.shape[0] // 2
    part = (part[:half] + shift(part[half:], swap=1)).reshape(4, -1, 256)
    grad_embed = part[0]
    for d in (1, 2, 3):
        grad_embed = grad_embed + shift(part[d].astype(bf16), dz=-d).astype(f32)
    emb_cot = grad_embed.astype(bf16)
    small = jnp.concatenate(
        [
            means * inv[:, None],
            jnp.concatenate([0.5 * jnp.sum(v[8:], (1, 2)) / (mix_weight * mix_var * (-2 * math.pi**2)),
                             0.5 / mix_var * jnp.sum(v[:8], (1, 2)), jnp.zeros((240,), f32)])[None],
            jnp.zeros((7, 256), f32),
        ],
        0,
    )
    series_all = series_z + [shift(s, swap=1) for s in series_z]
    slope, hid_out = late_pre(w_own, w_pick, series_all)
    sent = jnp.concatenate([emb_cot, *split(small, 2)], 0)
    cots = [sent] + [shift(sent, dz=d) for d in (1, 2, 3)]
    cots, slope, hid_out = lax.optimization_barrier((cots, slope, hid_out))
    cots = cots + [shift(c, swap=1) for c in cots]
    out = late_part(at, slope, hid_out, w_out, cots, series_all)
    out = x_sum(out, [shift(out[d], dx=d) for d in (1, 2, 3)])
    grad_in, grad_out, weights, varies, means = y_sum(out, [shift(out[d], dy=d) for d in (1, 2, 3)])
    return (grad_embed, grad_in, grad_out, weights, varies, means)


def solution(mesh):
    both = P(("row", "col"), None)
    return jax.shard_map(
        body,
        mesh=mesh,
        in_specs=(both, P(), P(), both, both, P(), P(), P()),
        out_specs=(both, P("row", "col"), both, P(), P(), P()),
        check_vma=False,
    )
```

```python
import functools
import math

import jax
import jax.numpy as jnp
import numpy as np
from jax import lax
from jax.experimental import pallas as pl
from jax.experimental.pallas import tpu as pltpu
from jax.sharding import PartitionSpec as P

f32, bf16 = jnp.float32, jnp.bfloat16
NT = (((1,), (1,)), ((), ()))
NN = (((1,), (0,)), ((), ()))


def mm(a, b, dims):
    return lax.dot_general(a, b, dims, preferred_element_type=f32)


def split(x, n):
    out = []
    for _ in range(n):
        h = lax.reduce_precision(x, 8, 7)
        out.append(h.astype(bf16))
        x = x - h
    return out


def rates(mix_var):
    return (-2 * math.pi**2 * math.log2(math.e)) * mix_var


HI = lax.Precision.HIGHEST
TN = (((0,), (0,)), ((), ()))


def sel_matrix():
    m = np.zeros((256, 128), np.float32)
    for q in range(8):
        for t, at in enumerate((64, 72, 88, 96)):
            m[16*(q//4) + 4*t + q%4, at+q] = 1
        m[32+q, 72+q] = 1; m[40+q, 80+q] = 1; m[48+q, 96+q] = 1; m[56+q, 104+q] = 1
    m[64:72, 112:115] = 1
    m[128+115:128+118, :] = 1
    return m


def prep2(emb, fa, fb, mw, mv, mmean):
    ef = emb.astype(f32)
    ang = 2*math.pi*lax.dot_general(ef, mmean, NT, precision=HI)
    c, s = jnp.cos(ang), jnp.sin(ang)
    n = jnp.sum(ef*ef, 1, keepdims=True)
    nh, nm, nl = split(n, 3)
    one = jnp.ones((emb.shape[0], 3), bf16)
    a = mw * (-2*math.pi**2) * mv
    ch, cl = split(c, 2); sh, sl = split(s, 2)
    ah, al = split(c*a, 2); bh, bl = split(s*a, 2)
    z = jnp.zeros((emb.shape[0], 10), bf16)
    colp = jnp.concatenate([emb*-2, fa, fb, ch, cl, ch, sh, sl, sh, nh, nm, nl, one, z], 1)
    rowp = jnp.concatenate([emb, fb, fa, ah, ah, al, bh, bh, bl, one, nh, nm, nl, z], 1)
    return rowp, colp


def halves(x):
    one = x.astype(bf16).astype(f32)
    return one, (x - one).astype(bf16).astype(f32)


def tile_kernel(TS, CE2, TR, TC, final, n_prev, rate_ref, sel_ref, mean_ref, row_ref, col_ref, *refs):
    prev, outs = refs[:n_prev], refs[n_prev:]
    if final:
        grad_ref, means_ref, v_ref = outs[:3]
    else:
        pulled_ref, rsum_ref, cs_ref, v_ref, rowc_s = outs[:5]
    outs = outs[3 if final else 5:]
    if prev:
        rowc_s = prev[4]
    elif final:
        rowc_s, outs = outs[0], outs[1:]
    (d0, d1, o0, o1, m0, m1, c0, c1, pulled_s, rsum_s, cs_s, cst_s, ni_s, nj_s) = outs
    HW = 128
    R, C = row_ref.shape[0], col_ref.shape[0]
    Q = rate_ref.shape[0]
    NC, NR = C // TC, R // TR
    N = NC * NR
    NS = TR // TS
    CW = min(TC, 256)
    lane = lax.broadcasted_iota(jnp.int32, (TS, 128), 1)
    def zero(*refs):
        for r in refs:
            r[...] = jnp.zeros_like(r)
    zero(d1, o1, m0, c0)
    if final:
        zero(means_ref)

    def load_sums(i):
        if prev:
            rows = pl.ds(pl.multiple_of(i * TR, TR), TR)
            pulled_s[...] = prev[0][rows, :]
            rsum_s[...] = prev[1][rows, :]
            cs_s[...] = prev[2][i]
        else:
            zero(pulled_s, rsum_s, cs_s)

    load_sums(0)
    if prev:
        v_ref[...] = prev[3][...]
    else:
        zero(v_ref)
    lr = lax.broadcasted_iota(jnp.int32, (TR, 128), 1)
    sub = lax.broadcasted_iota(jnp.int32, (16, TC), 0)

    def rowcol(t):
        t = jnp.clip(t, 0, N - 1)
        i, j = lax.div(t, NC), lax.rem(t, NC)
        return pl.multiple_of(i * TR, TR), pl.multiple_of(j * TC, TC)

    def products(t, d_s, o_s):
        r0, q0 = rowcol(t)
        cols = pl.ds(q0, TC)
        rows = pl.ds(r0, TR)

        def dist():
            norms = jnp.concatenate([ni_s[rows, :]] * (TC // 128), 1) + nj_s[0:1, cols]
            d_s[...] = norms + mm(row_ref[rows, :256], col_ref[cols, :256], NT)

        def outer():
            rtail = row_ref[rows, 256:384]
            keep = jnp.where((lr < 64) & (t < N), rtail, jnp.zeros_like(rtail))
            o_s[...] = mm(keep, col_ref[cols, 256:384], NT)

        return [dist, outer]

    def sums(t, damp_s, c_s):
        _, q0 = rowcol(t)
        cols = pl.ds(q0, TC)
        acc = [None, None]

        def waves(q):
            r = mm(cst_s[q, :, cols], damp_s[q], NT)
            h = q // 4
            acc[h] = r if acc[h] is None else acc[h] + r
            if q % 4 == 3:
                cs_s[16*h:16*h+16] += acc[h]

        def pull(h):
            M = TR
            rows = slice(h * M, (h + 1) * M)
            emb = col_ref[cols, :256]
            c = c_s[rows, :]
            chi = c.astype(bf16)
            pu = mm(chi, emb, NN)
            if CE2:
                pu = pu + mm((c - chi.astype(f32)).astype(bf16), emb, NN)
            pulled_s[rows, :] += pu
            rs = c[:, :128]
            for k in range(1, TC // 128):
                rs = rs + c[:, k*128:(k+1)*128]
            rsum_s[rows, :] += rs

        return [functools.partial(waves, q) for q in range(Q)], [functools.partial(pull, h) for h in range(1)]

    def stage(t, da, oa, ds, os, ms, cs, mc, cc_):
        first = products(t, da, oa)
        waves, pulls = sums(t - 2, mc, cc_)
        r0, q0 = rowcol(t - 1)
        for s in range(NS):
            rs = slice(s * TS, (s + 1) * TS)
            lhs = rowc_s[pl.ds(pl.multiple_of((r0 + s * TS) * Q, TS * Q), Q*TS), :]
            for cc in range(TC // CW):
                cols = slice(cc*CW, (cc+1)*CW)
                cos = mm(lhs, col_ref[pl.ds(q0 + cc*CW, CW), 256:384], NT)
                for hh in range(CW // HW):
                    sl = slice(hh*HW, (hh+1)*HW)
                    hcols = slice(cc*CW + hh*HW, cc*CW + (hh+1)*HW)
                    d = ds[rs, hcols]
                    o = os[rs, hcols]
                    c = None
                    for q in range(Q):
                        damp = o * jnp.exp2(d * rate_ref[q])
                        ms[q, rs, hcols] = damp.astype(bf16)
                        even = damp * cos[q*TS:(q+1)*TS, sl]
                        c = even if c is None else c + even
                        ed = even * d
                        x = ed[:, :128]
                        for k in range(1, HW // 128):
                            x = x + ed[:, k*128:(k+1)*128]
                        x = x.reshape(TS//8, 8, 128).sum(0)
                        v_ref[q] += x
                        v_ref[Q + q] += even.reshape(TS//8, 8, 128).sum(0)
                    cs[rs, hcols] = c
            for k in range(-(-Q // NS)):
                if waves:
                    waves.pop(0)()
            if s % max(1, NS // 2) == 0 and first:
                first.pop(0)()
            if (s % max(1, NS // 2) == 1 or NS == 2) and pulls:
                pulls.pop(0)()
        for f in first + waves + pulls:
            f()

    def end_rows(t):
        @pl.when((t >= 0) & (lax.rem(t, NC) == NC - 1))
        def _():
            r0, _ = rowcol(t)
            rows = pl.ds(r0, TR)
            if final:
                ef = row_ref[rows, :256].astype(f32)
                cs = cs_s[...]
                wc = jnp.concatenate([cs[0:4] + cs[4:8], cs[16:20] + cs[20:24]], 0)
                ws = jnp.concatenate([cs[8:12] + cs[12:16], cs[24:28] + cs[28:32]], 0)
                rt = mm(sel_ref[32:64], row_ref[rows, 256:384], NT)
                ac = rt[0:8] + rt[8:16]
                as_ = rt[16:24] + rt[24:32]
                spin = as_ * wc - ac * ws
                rowsum = jnp.sum(rsum_s[...], 1, keepdims=True)
                one, two = halves(spin)
                m_one, m_two = halves(mean_ref[...])
                pad = jnp.zeros_like(one)
                back = mm(jnp.concatenate([one, two, one, pad], 0).astype(bf16),
                          jnp.concatenate([m_one, m_one, m_two, jnp.zeros_like(m_one)], 0).astype(bf16), TN)
                grad_ref[rows, :] = (2.0 * rowsum * ef + pulled_s[...] + back).astype(grad_ref.dtype)
                both = mm(jnp.concatenate([one, two], 0).astype(bf16), row_ref[rows, :256], NN)
                means_ref[...] += both[:8] + both[8:]
            else:
                pulled_ref[rows, :] = pulled_s[...]
                rsum_ref[rows, :] = rsum_s[...]
                cs_ref[lax.div(t, NC)] = cs_s[...]
            load_sums(jnp.minimum(lax.div(t, NC) + 1, NR - 1))

    if not prev:
        for s in range(R // TS):
            x = row_ref[s*TS:(s+1)*TS, 256:384]
            for q in range(Q):
                keep = (lane >= 64) & (lane < 112) & (lane % 8 == q)
                rowc_s[(s*Q+q)*TS:(s*Q+q+1)*TS, :] = jnp.where(keep, x, jnp.zeros_like(x))
    for k in range(C // TC):
        cst = mm(sel_ref[:32], col_ref[k*TC:(k+1)*TC, 256:384], NT)
        for q in range(Q):
            keep = cst[16*(q//4):16*(q//4)+16]
            cst_s[q, :, k*TC:(k+1)*TC] = jnp.where(sub % 4 == q % 4, keep, 0.0).astype(bf16)
        nj_s[:, k*TC:(k+1)*TC] = mm(sel_ref[64:72], col_ref[k*TC:(k+1)*TC, 256:384], NT)
    for k in range(R // TR):
        ni_s[k*TR:(k+1)*TR, :] = mm(row_ref[k*TR:(k+1)*TR, 256:384], sel_ref[128:256], NN)

    def pair(h, _):
        t = 2 * h
        stage(t, d0, o0, d1, o1, m1, c1, m0, c0)
        stage(t + 1, d1, o1, d0, o0, m0, c0, m1, c1)
        end_rows(t - 1)
        return 0
    lax.fori_loop(0, (N + 2) // 2, pair, 0)

def tile(rate, mean_s, rowp, colp, prev=(), final=True, TR=256, TC=256, TS=64, CE2=False):
    R, C, Q = rowp.shape[0], colp.shape[0], rate.shape[0]
    assert (R // TR) * (C // TC) % 2 == 0
    vm = pl.BlockSpec(memory_space=pltpu.VMEM)
    sc = lambda *s: pltpu.VMEM(s, f32)
    shape = lambda *dims: jax.ShapeDtypeStruct(dims, f32)
    if final:
        shapes = [shape(R, 256), shape(8, 256), shape(2 * Q, 8, 128)]
    else:
        shapes = [shape(R, 256), shape(R, 128), shape(R // TR, 32, TR), shape(2 * Q, 8, 128),
                  jax.ShapeDtypeStruct((R * Q, 128), bf16)]
    return pl.pallas_call(
        functools.partial(tile_kernel, TS, CE2, TR, TC, final, len(prev)),
        in_specs=[pl.BlockSpec(memory_space=pltpu.SMEM), vm, vm, vm, vm] + [vm] * len(prev),
        out_specs=[vm] * len(shapes),
        out_shape=shapes,
        scratch_shapes=([pltpu.VMEM((R*Q, 128), bf16)] if final and not prev else []) + [sc(TR, TC), sc(TR, TC), sc(TR, TC), sc(TR, TC),
                        pltpu.VMEM((Q, TR, TC), bf16), pltpu.VMEM((Q, TR, TC), bf16), sc(TR, TC), sc(TR, TC),
                        sc(TR, 256), sc(TR, 128), sc(32, TR), pltpu.VMEM((Q, 16, C), bf16), sc(R, 128), sc(8, C)],
        cost_estimate=pl.CostEstimate(flops=20 * R * C * 256, bytes_accessed=4 * 10**6, transcendentals=R * C * Q),
        compiler_params=pltpu.CompilerParams(vmem_limit_bytes=20 << 20),
        name="tile",
    )(rate, jnp.asarray(sel_matrix(), bf16), mean_s, rowp, colp, *prev)


def pre_kernel(w_ref, wh_ref, *refs):
    pieces, (slope_ref, hid_ref) = refs[:-2], refs[-2:]
    for p in range(0, len(pieces), 2):
        two = jnp.concatenate([pieces[p][...], pieces[p+1][...]], 0)
        n = two.shape[0]
        cols = slice(p * n // 2, (p + 2) * n // 2)
        pre = mm(two, w_ref[...], NN)
        sig = jax.nn.sigmoid(pre)
        slope_ref[:, cols] = (sig * (1.0 + pre * (1.0 - sig))).T
        pre = mm(two, wh_ref[...], NN)
        hid_ref[:, cols] = (pre * jax.nn.sigmoid(pre)).T.astype(bf16)


def late_pre(w_own, w_pick, pieces):
    vm = pl.BlockSpec(memory_space=pltpu.VMEM)
    tok = sum(p.shape[0] for p in pieces)
    return pl.pallas_call(
        pre_kernel,
        in_specs=[vm] * (2 + len(pieces)),
        out_specs=[vm, vm],
        out_shape=[jax.ShapeDtypeStruct((w_own.shape[1], tok), f32), jax.ShapeDtypeStruct((w_pick.shape[1], tok), bf16)],
        cost_estimate=pl.CostEstimate(flops=4 * 10**9, bytes_accessed=6 * 10**6, transcendentals=400000),
        compiler_params=pltpu.CompilerParams(vmem_limit_bytes=20 << 20),
        name="pre",
    )(w_own, w_pick, *pieces)


def pair_split(x):
    h = x.astype(bf16)
    return h, (x - h.astype(f32)).astype(bf16)


def part_kernel(own, n, at_ref, slope_ref, hid_ref, w_ref, *refs):
    cots, pieces, (out_ref,) = refs[:n], refs[n:2*n], refs[2*n:]
    core, x, y, z = at_ref[0], at_ref[1], at_ref[2], at_ref[3]
    wide = slope_ref.shape[0]
    cot = jnp.concatenate([c[:own, :] for c in cots], 0)
    small = cots[0][own:own+16, :].astype(f32) + cots[0][own+16:own+32, :].astype(f32)
    for c in cots[1:]:
        small = small + (c[own:own+16, :].astype(f32) + c[own+16:own+32, :].astype(f32))
    hi, lo = pair_split(small)
    for k, part in enumerate((hi, lo)):
        for dest in range(4):
            out_ref[dest, 576+32*k:592+32*k, :] = part[:, :128]
            out_ref[dest, 592+32*k:608+32*k, :] = part[:, 128:]
    back = mm(w_ref[pl.ds(pl.multiple_of(z * wide, wide), wide), :], cot, NT)
    d = (back * slope_ref[...]).astype(bf16)
    grad_out = mm(hid_ref[...], cot, NN)
    for m in range(8):
        feats = pl.ds(pl.multiple_of((2 * m + core) * 128, 128), 128)
        g = mm(d, jnp.concatenate([p[:, feats] for p in pieces], 0), NN)
        sx = lax.rem(m % 4 - x + 4, 4)
        for h in range(2):
            sy = lax.rem(2 * h + m // 4 - y + 4, 4)
            base = pl.multiple_of(sy * 144, 16)
            out_ref[sx, pl.ds(base, 128), :] = g[h*128:(h+1)*128].astype(bf16)
            o = grad_out[16*m+8*h:16*m+8*h+8]
            out_ref[sx, pl.ds(base + 128, 16), :] = jnp.concatenate([o[:, :128], o[:, 128:]], 0).astype(bf16)


def late_part(at, slope, hid_out, w_out, cots, pieces):
    vm = pl.BlockSpec(memory_space=pltpu.VMEM)
    n = len(pieces)
    return pl.pallas_call(
        functools.partial(part_kernel, pieces[0].shape[0], n),
        in_specs=[pl.BlockSpec(memory_space=pltpu.SMEM)] + [vm] * (3 + 2 * n),
        out_specs=vm,
        out_shape=jax.ShapeDtypeStruct((4, 640, 128), bf16),
        cost_estimate=pl.CostEstimate(flops=2 * 10**9, bytes_accessed=6 * 10**6, transcendentals=0),
        compiler_params=pltpu.CompilerParams(vmem_limit_bytes=20 << 20),
        name="part",
    )(at, slope, hid_out, w_out, *cots, *pieces)


def add_kernel(first_ref, *refs):
    got, out_ref = refs[:3], refs[3]
    for dest in range(4):
        rows = slice(144 * dest, 144 * dest + 144)
        total = first_ref[0, rows].astype(f32)
        for g in got:
            total = total + g[rows].astype(f32)
        out_ref[dest, :144, :] = total.astype(bf16)
    value = first_ref[0, 576:608].astype(f32) + first_ref[0, 608:640].astype(f32)
    for g in got:
        value = value + (g[576:608].astype(f32) + g[608:640].astype(f32))
    hi, lo = pair_split(value)
    for dest in range(4):
        out_ref[dest, 144:176, :] = hi
        out_ref[dest, 176:208, :] = lo


def x_sum(out, got):
    vm = pl.BlockSpec(memory_space=pltpu.VMEM)
    return pl.pallas_call(
        add_kernel,
        grid=(1,),
        in_specs=[pl.BlockSpec((1, 640, 128), lambda i: (0, 0, 0))] + [vm] * 3,
        out_specs=vm,
        out_shape=jax.ShapeDtypeStruct((4, 208, 128), bf16),
        compiler_params=pltpu.CompilerParams(vmem_limit_bytes=6 << 20),
        name="x_sum",
    )(out, *got)


def end_kernel(first_ref, *refs):
    got, (in_ref, out_ref, weight_ref, var_ref, mean_ref) = refs[:3], refs[3:]
    total = first_ref[0].astype(f32)
    for g in got:
        total = total + g[...].astype(f32)
    in_ref[...] = total[:128].T
    out_ref[:, :128] = total[128:136]
    out_ref[:, 128:] = total[136:144]
    value = total[144:176] + total[176:208]
    mean_ref[:, :128] = value[:8]
    mean_ref[:, 128:] = value[16:24]
    weight_ref[...] = value[8, :8]
    var_ref[...] = value[8, 8:16]


def y_sum(out, got):
    vm = pl.BlockSpec(memory_space=pltpu.VMEM)
    return pl.pallas_call(
        end_kernel,
        grid=(1,),
        in_specs=[pl.BlockSpec((1, 208, 128), lambda i: (0, 0, 0))] + [vm] * 3,
        out_specs=[vm] * 5,
        out_shape=[jax.ShapeDtypeStruct((128, 128), f32), jax.ShapeDtypeStruct((8, 256), f32), jax.ShapeDtypeStruct((8,), f32),
                   jax.ShapeDtypeStruct((8,), f32), jax.ShapeDtypeStruct((8, 256), f32)],
        compiler_params=pltpu.CompilerParams(vmem_limit_bytes=6 << 20),
        name="y_sum",
    )(out, *got)


BOTH = ("row", "col")


def device_at(core, x, y, z):
    x, y, z = x % 4, y % 4, z % 4
    return (((y % 2) * 4 + x) * 2 + core) * 8 + z * 2 + y // 2


def shift(v, dx=0, dy=0, dz=0, swap=0):
    pairs = [(device_at(k, x, y, z), device_at(k ^ swap, x + dx, y + dy, z + dz))
             for k in range(2) for x in range(4) for y in range(4) for z in range(4)]
    return lax.ppermute(v, BOTH, sorted(pairs))


def fan(v, axis):
    return [shift(v, **{axis: d}) for d in (3, 2, 1)]


def body(series, w_in, w_out, factor_a, factor_b, mix_weight, mix_var, mix_mean):
    row, col = lax.axis_index("row"), lax.axis_index("col")
    core, x, z = lax.rem(row, 2), lax.rem(lax.div(row, 2), 4), lax.div(col, 2)
    y = 2 * lax.rem(col, 2) + lax.div(row, 8)
    at = jnp.stack([core, x, y, z]).astype(jnp.int32)
    pre = jnp.dot(series, w_in, preferred_element_type=f32)
    hidden = jax.nn.silu(pre).astype(bf16)
    emb = jnp.dot(hidden, w_out, preferred_element_type=f32).astype(bf16)
    rowp, colp = prep2(emb, factor_a, factor_b, mix_weight, mix_var, mix_mean)
    rows = jnp.concatenate([rowp] + fan(rowp, "dz"), 0)
    rows, series_late = lax.optimization_barrier((rows, series))
    series_z = [series_late] + [shift(series_late, dz=d) for d in (1, 2, 3)]
    near = jnp.concatenate([colp] + fan(colp, "dy"), 0)
    rows = jnp.concatenate([rows, shift(rows, swap=1)], 0)
    near, w_in_late = lax.optimization_barrier((near, w_in))
    far = jnp.concatenate(fan(near, "dx"), 0)
    inv = 1.0 / (math.pi * mix_var)
    rate, mean_s = rates(mix_var), mix_mean * inv[:, None]
    sums = tile(rate, mean_s, rows, near, final=False)
    hid = w_in.shape[1]
    wide = hid // 4
    k = jnp.arange(hid // 8)
    ids = (2 * (k // 16) + core) * 64 + z * 16 + k % 16
    pick = (jnp.arange(hid)[:, None] == ids[None, :]).astype(bf16)
    w_pick = jnp.dot(w_in_late, pick, preferred_element_type=f32).astype(bf16)
    w_own = lax.dynamic_slice_in_dim(w_in_late, z * wide, wide, 1)
    rows, far, sums, w_own, w_pick = lax.optimization_barrier((rows, far, sums, w_own, w_pick))
    part, means, v = tile(rate, mean_s, rows, far, prev=sums)
    series_z, part = lax.optimization_barrier((series_z, part))
    half = part.shape[0] // 2
    part = (part[:half] + shift(part[half:], swap=1)).reshape(4, -1, 256)
    grad_embed = part[0]
    for k, d in enumerate((3, 2, 1)):
        grad_embed = grad_embed + shift(part[k + 1].astype(bf16), dz=-d).astype(f32)
    emb_cot = grad_embed.astype(bf16)
    small = jnp.concatenate(
        [
            means * inv[:, None],
            jnp.concatenate([0.5 * jnp.sum(v[8:], (1, 2)) / (mix_weight * mix_var * (-2 * math.pi**2)),
                             0.5 / mix_var * jnp.sum(v[:8], (1, 2)), jnp.zeros((240,), f32)])[None],
            jnp.zeros((7, 256), f32),
        ],
        0,
    )
    series_all = series_z + [shift(s, swap=1) for s in series_z]
    slope, hid_out = late_pre(w_own, w_pick, series_all)
    sent = jnp.concatenate([emb_cot, *split(small, 2)], 0)
    cots = [sent] + [shift(sent, dz=d) for d in (1, 2, 3)]
    cots, slope, hid_out = lax.optimization_barrier((cots, slope, hid_out))
    cots = cots + [shift(c, swap=1) for c in cots]
    out = late_part(at, slope, hid_out, w_out, cots, series_all)
    out = x_sum(out, [shift(out[d], dx=d) for d in (1, 2, 3)])
    grad_in, grad_out, weights, varies, means = y_sum(out, [shift(out[d], dy=d) for d in (1, 2, 3)])
    return (grad_embed, grad_in, grad_out, weights, varies, means)


def solution(mesh):
    both = P(("row", "col"), None)
    return jax.shard_map(
        body,
        mesh=mesh,
        in_specs=(both, P(), P(), both, both, P(), P(), P()),
        out_specs=(both, P("row", "col"), both, P(), P(), P()),
        check_vma=False,
    )
```
